256 devices in a mesh: tile: 64 (over x, z, core), mem: 4 (over y).
Axes of the slice: x: 4, y: 4, z: 8, core: 2. Of those that a mesh axis runs over, the one named last changes fastest.
Arguments:
- control: float32 [64, 64, 32768], P('mem', None, 'tile'), may hold values from -8 to 8
- ensemble: bfloat16 [64, 5, 64, 32768], P('mem', None, None, 'tile'), may hold values from -6 to 6
- jacobian: bfloat16 [640, 320], replicated, may hold values from -0.3125 to 0.3125
- send_columns: int32 [256, 64, 2], P(('tile', 'mem')), may hold values from 0 to 127, as said below
- received_counts: int32 [256, 64], P(('tile', 'mem')), may hold values from 0 to 2, as said below
- observed_channel: int32 [256, 64, 2, 128], P(('tile', 'mem')), may hold values from 0 to 639
- innovation: float32 [256, 64, 2, 128], P(('tile', 'mem')), may hold values from -1.5 to 1.5
- error_weight: float32 [256, 64, 2, 128], P(('tile', 'mem')), may hold values from 1 to 10
Outputs:
- gradient: float32 [64, 64, 32768], P('mem', None, 'tile')
- departures: float32 [256, 64, 2, 128], P(('tile', 'mem'))
The draws below stay inside these ranges and needn't reach their ends.
Inputs may be any that keep to these rules, and one draw needn't show every extreme that they name: `send_columns`: entry [d, t, j] is a column within the 128 columns of block k of strip s, where d = s * 4 + k; the entries of one row d are distinct. `received_counts`: entry [e, s] counts the used slots, from the first, of the 2 slots that device e receives from tile s. In each mem group one owner receives 2 from every source tile.
All inputs are finite; a program needn't handle non-finite values.
Results may differ from the reference program's by a relative error of at most 0.01.
Values may be sent and summed in bfloat16 or wider, within the bound.
No kernel may reach another device: no remote copies, remote signals or barrier semaphores. Data moves between devices by JAX's collectives and lax.ppermute only.
A program may use at most 64 MiB of HBM per device.

```python
import math
import jax
import jax.numpy as jnp
from jax import lax

NY = 64
LV = 64
V = 5
CH = 640
NCH = 128
CAP = 2
MEMBERS = 64
MEM_GROUPS = 4
OWNERS = 64
PLACES = 256
NX = 512
TILE_COLS = 512
BLOCK_COLS = 128
NCOLS = 32768
STATE = 320


def routing_tables(key):
    base = jax.random.fold_in(key, 7)
    key_heavy, key_level, key_raw, key_perm = jax.random.split(base, 4)
    groups = PLACES // OWNERS
    heavy = jax.random.randint(key_heavy, (groups,), 0, OWNERS)
    level = jax.random.randint(key_level, (OWNERS,), 0, 4)
    raw_counts = jax.random.randint(key_raw, (PLACES, OWNERS), 0, 4)
    counts = jnp.minimum(jnp.minimum(raw_counts, level[None, :]), CAP)
    group_of = jnp.arange(PLACES) % groups
    is_heavy = jnp.arange(OWNERS)[None, :] == heavy[group_of][:, None]
    counts = jnp.where(is_heavy, CAP, counts).astype(jnp.int32)
    perm_keys = jax.random.split(key_perm, PLACES)
    perms = jax.vmap(lambda sub_key: jax.random.permutation(sub_key, BLOCK_COLS))(perm_keys)
    slot_ids = jnp.arange(OWNERS)[:, None] * CAP + jnp.arange(CAP)[None, :]
    sending = perms[:, slot_ids].astype(jnp.int32)
    received = jnp.transpose(counts.reshape(OWNERS, groups, OWNERS), (2, 1, 0)).reshape(PLACES, OWNERS)
    return (sending, received.astype(jnp.int32))


def draw_send_columns(key, part):
    return routing_tables(key)[0]


def draw_received_counts(key, part):
    return routing_tables(key)[1]


def draw_control(key, part):
    base = jax.random.fold_in(key, 11)
    key_noise, key_amplitude = jax.random.split(base, 2)
    noise = jnp.clip(jax.random.normal(key_noise, (MEMBERS, LV, NCOLS), jnp.float32), -5.0, 5.0)
    amplitude = jax.random.uniform(key_amplitude, (MEMBERS, LV, 1), jnp.float32, 2.5, 3.0)
    row_index = jnp.arange(NCOLS, dtype=jnp.int32) // NY
    row_sign = 1.0 - 2.0 * (row_index % 2).astype(jnp.float32)
    return (noise + amplitude * row_sign[None, None, :]).astype(jnp.float32)


def touch_ends(values, own_key, smallest, high):
    shape = values.shape
    index_at = [jax.random.randint(jax.random.fold_in(own_key, axis), (), 0, shape[axis]) for axis in range(len(shape))]
    values = values.at[tuple(index_at)].set(smallest)
    longest = shape.index(max(shape))
    index_at[longest] = (index_at[longest] + 1) % shape[longest]
    return values.at[tuple(index_at)].set(high)


def steps_of(own_key, shape, pieces, least, high):
    def one(axis_at, parts):
        heights = jax.random.uniform(jax.random.fold_in(jax.random.fold_in(own_key, 6), axis_at), (parts,), jnp.float32, least / len(pieces), high / len(pieces))
        return jnp.repeat(jnp.exp(heights), shape[axis_at] // parts).reshape((-1,) + (1,) * (len(shape) - axis_at - 1))

    level = one(*pieces[0])
    for cut in pieces[1:]:
        level = level * one(*cut)
    return level


def normal_values(stream_key, dims, scale, most, cuts=(), kind=jnp.bfloat16):
    entries = jax.random.normal(stream_key, dims, jnp.float32) * scale
    if len(cuts) > 0:
        entries = steps_of(stream_key, dims, cuts, -0.22, 0.18) * entries
    return jnp.clip(entries, min=-most, max=most).astype(kind)


def setup_inputs(seed: int = 0) -> dict:
    seeds = jax.random.split(jax.random.key(seed), 9)
    return {
        "control": draw_control(jax.random.fold_in(seeds[8], 71), 0),
        "ensemble": normal_values(seeds[1], (MEMBERS, V, LV, NCOLS), 1.0, 6.0, ((0, 4), (3, 64))),
        "jacobian": normal_values(seeds[2], (CH, STATE), STATE ** -0.5, 0.3125),
        "send_columns": draw_send_columns(jax.random.fold_in(seeds[8], 71), 0),
        "received_counts": draw_received_counts(jax.random.fold_in(seeds[8], 71), 0),
        "observed_channel": touch_ends(jax.random.randint(seeds[5], (PLACES, OWNERS, CAP, NCH), 0, CH), jax.random.fold_in(seeds[5], 1), 0, CH - 1).astype(jnp.int32),
        "innovation": normal_values(seeds[6], (PLACES, OWNERS, CAP, NCH), 0.25, 1.5, ((0, 256),), jnp.float32),
        "error_weight": jnp.clip(jnp.exp(math.log(10.0) - 2.3025851 * jax.random.uniform(seeds[7], (PLACES, OWNERS, CAP, NCH), jnp.float32) ** steps_of(seeds[7], (PLACES, OWNERS, CAP, NCH), ((0, 256),), -0.2, 0.2)), 1.0, 10.0),
    }


diffusion_coef = 0.2

def apply_diffusion_operator(state_field):
    padded = jnp.pad(state_field, ((0, 0), (1, 1), (1, 1)))
    beside = padded[:, 2:, 1:-1] + padded[:, :-2, 1:-1] + padded[:, 1:-1, 2:] + padded[:, 1:-1, :-2]
    return state_field + diffusion_coef * (beside - 4.0 * state_field)

def quadruple_sweeps(member_field):
    grid = member_field.reshape(LV, NX, NY)
    for sweep_turn in range(4):
        grid = apply_diffusion_operator(grid)
    return grid.reshape(LV, NCOLS)

def reference(control, ensemble, jacobian, send_columns, received_counts, observed_channel, innovation, error_weight):
    member_scale = 1.0 / math.sqrt(MEMBERS)
    localized_member_field = lax.map(quadruple_sweeps, control)
    localization_weights = localized_member_field.astype(jnp.bfloat16)

    def accumulate(carry, pair):
        weights_one, member_one = pair
        return (carry + weights_one.astype(jnp.float32)[None] * member_one.astype(jnp.float32), None)
    summed, _ = lax.scan(accumulate, jnp.zeros((V, LV, NCOLS), jnp.float32), (localization_weights, ensemble))
    increment = (summed * member_scale).astype(jnp.bfloat16).reshape(STATE, NCOLS)
    device_ids = jnp.arange(PLACES, dtype=jnp.int32)
    offsets = device_ids // MEM_GROUPS * TILE_COLS + device_ids % MEM_GROUPS * BLOCK_COLS
    carried = (offsets[:, None, None] + send_columns).astype(jnp.int32)
    columns_first = jnp.transpose(increment)
    outgoing = jnp.take(columns_first, carried.reshape(-1), axis=0)
    outgoing = outgoing.reshape(OWNERS, MEM_GROUPS, OWNERS, CAP, STATE)
    incoming = jnp.transpose(outgoing, (2, 1, 0, 3, 4)).reshape(PLACES * OWNERS * CAP, STATE)
    model_channels = jnp.dot(incoming, jnp.transpose(jacobian), preferred_element_type=jnp.float32)
    model_channels = model_channels.reshape(PLACES, OWNERS, CAP, CH)
    evolved = jnp.take_along_axis(model_channels, observed_channel, axis=3)
    filled = jnp.arange(CAP, dtype=jnp.int32)[None, None, :, None] < received_counts[:, :, None, None]
    departures = jnp.where(filled, evolved - innovation, 0.0)
    weighted = error_weight * departures
    row_count = PLACES * OWNERS * CAP
    row_ids = jnp.broadcast_to(jnp.arange(row_count, dtype=jnp.int32)[:, None], (row_count, NCH))
    channel_adjoint = jnp.zeros((row_count, CH), jnp.float32).at[row_ids, observed_channel.reshape(row_count, NCH)].add(weighted.reshape(row_count, NCH))
    channel_adjoint = channel_adjoint.astype(jnp.bfloat16)
    column_adjoint = jnp.dot(channel_adjoint, jacobian, preferred_element_type=jnp.float32).astype(jnp.bfloat16)
    returned = column_adjoint.reshape(OWNERS, MEM_GROUPS, OWNERS, CAP, STATE)
    returned = jnp.transpose(returned, (2, 1, 0, 3, 4)).reshape(row_count, STATE)
    adjoint_first = jnp.zeros((NCOLS, STATE), jnp.float32).at[carried.reshape(-1)].add(returned.astype(jnp.float32))
    analysis_increment_adjoint = jnp.transpose(adjoint_first.astype(jnp.bfloat16)).reshape(V, LV, NCOLS)

    def member_gradient(member_one):
        member_adjoint = lax.optimization_barrier(jnp.sum(member_one.astype(jnp.float32) * analysis_increment_adjoint.astype(jnp.float32), axis=0)) * member_scale
        return quadruple_sweeps(member_adjoint)
    gradient = lax.map(member_gradient, ensemble)
    return (gradient, departures)
```

```python
import functools
import math

import jax
import jax.numpy as jnp
import numpy as np
from jax import lax
from jax.experimental import pallas as pl
from jax.experimental.pallas import tpu as pltpu
from jax.sharding import PartitionSpec as P

NY = 64
SWEEPS = 4
DIFFUSION = 0.2
HALF = SWEEPS * NY

CONTROL_STEP = 8.0 / 32704.0
INNOVATION_STEP = 1.5 / 32700.0
WEIGHT_STEP = 10.0 / 32700.0

F32 = jnp.float32
BF16 = jnp.bfloat16
I16 = jnp.int16
I32 = jnp.int32


def sweep_matrices():
    y_part = (1.0 - 4.0 * DIFFUSION) * np.eye(NY) + DIFFUSION * (
        np.eye(NY, k=1) + np.eye(NY, k=-1)
    )
    powers = [np.linalg.matrix_power(y_part, n) for n in range(SWEEPS + 1)]
    by_distance = [np.zeros((NY, NY)) for _ in range(SWEEPS + 1)]
    for k in range(SWEEPS + 1):
        for ups in range(k + 1):
            distance = 2 * ups - k
            if distance >= 0:
                by_distance[distance] = by_distance[distance] + (
                    math.comb(SWEEPS, k)
                    * DIFFUSION**k
                    * math.comb(k, ups)
                    * powers[SWEEPS - k]
                )

    def block(distance_of, image_of=None):
        full = np.zeros((HALF, HALF))
        for xi in range(SWEEPS):
            for xo in range(SWEEPS):
                piece = np.zeros((NY, NY))
                if distance_of(xi, xo) <= SWEEPS:
                    piece = piece + by_distance[distance_of(xi, xo)]
                if image_of is not None and image_of(xi, xo) <= SWEEPS:
                    piece = piece - by_distance[image_of(xi, xo)]
                full[xi * NY : (xi + 1) * NY, xo * NY : (xo + 1) * NY] = piece
        return full

    last = SWEEPS - 1
    same = lambda xi, xo: abs(xi - xo)
    blocks = [
        block(same, lambda xi, xo: xi + xo + 2),
        block(same),
        block(same, lambda xi, xo: (last - xi) + (last - xo) + 2),
        block(lambda xi, xo: xo + SWEEPS - xi),
        block(lambda xi, xo: xi + SWEEPS - xo),
    ]
    stacked = np.stack(blocks).astype(np.float32)
    high = stacked.astype(jnp.bfloat16)
    low = (stacked - high.astype(np.float32)).astype(jnp.bfloat16)
    return np.stack([high, low], axis=1)


def split_high_low(values):
    high = values.astype(BF16)
    return high, (values - high.astype(F32)).astype(BF16)


def mm(a, b):
    return jnp.dot(a, b, preferred_element_type=F32)


def mm_nt(a, b):
    return lax.dot_general(a, b, (((1,), (1,)), ((), ())), preferred_element_type=F32)


def params(**extra):
    return pltpu.CompilerParams(vmem_limit_bytes=48 * 1024 * 1024, **extra)


def cost(flops, bytes_accessed):
    return pl.CostEstimate(flops=flops, bytes_accessed=bytes_accessed, transcendentals=0)


def sweep_own_kernel(edge_ref, x_ref, t_left, t_right, t_after, t_before, o_ref):
    left, right = x_ref[:, :HALF], x_ref[:, HALF:]
    left_high, left_low = split_high_low(left)
    right_high, right_low = split_high_low(right)

    def apply(high, low, t_ref):
        return mm(high, t_ref[0, 0]) + mm(low, t_ref[0, 0]) + mm(high, t_ref[0, 1])

    o_ref[:, :HALF] = apply(left_high, left_low, t_left) + apply(right_high, right_low, t_before)
    o_ref[:, HALF:] = apply(right_high, right_low, t_right) + apply(left_high, left_low, t_after)


def sweep_own(edges, field, matrices):
    rows, columns = field.shape
    step = 256
    t_spec = lambda pick: pl.BlockSpec((1, 2, HALF, HALF), pick)
    return pl.pallas_call(
        sweep_own_kernel,
        out_shape=jax.ShapeDtypeStruct((rows, columns), F32),
        grid_spec=pltpu.PrefetchScalarGridSpec(
            num_scalar_prefetch=1,
            grid=(rows // step,),
            in_specs=[
                pl.BlockSpec((step, columns), lambda i, e: (i, 0)),
                t_spec(lambda i, e: (e[0], 0, 0, 0)),
                t_spec(lambda i, e: (e[1], 0, 0, 0)),
                t_spec(lambda i, e: (3, 0, 0, 0)),
                t_spec(lambda i, e: (4, 0, 0, 0)),
            ],
            out_specs=pl.BlockSpec((step, columns), lambda i, e: (i, 0)),
        ),
        compiler_params=params(),
        cost_estimate=cost(2 * 6 * rows * columns * HALF, 10 * rows * columns),
        name="sweep_own",
    )(edges, field, matrices, matrices, matrices, matrices)


def member_sum_kernel(scale, own_ref, low_ref, high_ref, ens_ref, t_after, t_before, o_ref):
    members, levels, columns = own_ref.shape
    variables = ens_ref.shape[1]
    blocks, width = o_ref.shape[0], o_ref.shape[3]
    half_blocks = blocks // 2

    def from_halo(halo_ref, t_ref):
        coded = halo_ref[...].reshape(members * levels, HALF).astype(I32)
        upper = (coded >> 8).astype(F32).astype(BF16)
        lower = (coded & 255).astype(F32).astype(BF16)
        upper_part = mm(upper, t_ref[0, 0]) + mm(upper, t_ref[0, 1])
        lower_part = mm(lower, t_ref[0, 0])
        total = (upper_part * 256.0 + lower_part) * CONTROL_STEP
        return total.reshape(members, levels, HALF)

    halos = [from_halo(low_ref, t_after), from_halo(high_ref, t_before)]
    for k in range(blocks):
        offset = (k % half_blocks) * width
        halo = halos[k // half_blocks][:, :, offset : offset + width]
        weights = own_ref[:, :, k * width : (k + 1) * width] + halo
        weights = weights.astype(BF16).astype(F32)
        for v in range(variables):
            total = None
            for m in range(members):
                term = weights[m] * ens_ref[m, v, :, k * width : (k + 1) * width].astype(F32)
                total = term if total is None else total + term
            o_ref[k, v] = (total * scale).astype(BF16)


def member_sum(own, from_low, from_high, ensemble, matrices, scale, blocks):
    members, variables, levels, columns = ensemble.shape
    step = 16
    width = columns // blocks
    return pl.pallas_call(
        functools.partial(member_sum_kernel, scale),
        out_shape=jax.ShapeDtypeStruct((blocks, variables, levels, width), BF16),
        grid=(levels // step,),
        in_specs=[
            pl.BlockSpec((members, step, columns), lambda i: (0, i, 0)),
            pl.BlockSpec((members, step, HALF), lambda i: (0, i, 0)),
            pl.BlockSpec((members, step, HALF), lambda i: (0, i, 0)),
            pl.BlockSpec((members, variables, step, columns), lambda i: (0, 0, i, 0)),
            pl.BlockSpec((1, 2, HALF, HALF), lambda i: (3, 0, 0, 0)),
            pl.BlockSpec((1, 2, HALF, HALF), lambda i: (4, 0, 0, 0)),
        ],
        out_specs=pl.BlockSpec((blocks, variables, step, width), lambda i: (0, 0, i, 0)),
        compiler_params=params(),
        cost_estimate=cost(
            2 * 3 * members * levels * columns * HALF, 2 * ensemble.size + 6 * own.size
        ),
        name="member_sum",
    )(own, from_low, from_high, ensemble, matrices, matrices)


def obs_tables_kernel(obs_ref, w_ref, b_ref):
    slots, width = obs_ref.shape[0], obs_ref.shape[2]
    groups = w_ref.shape[0]
    group_id = lax.broadcasted_iota(I32, (8, width), 0)
    lane_id = lax.broadcasted_iota(I32, (width, width), 0)

    def one(slot):
        row = obs_ref[slot].astype(I32)
        channel = row[0:1]
        innovation = row[1:2].astype(F32) * INNOVATION_STEP
        weight = row[2:3].astype(F32) * WEIGHT_STEP
        in_group = jnp.broadcast_to(channel >> 7, (8, width)) == group_id
        one_hot = jnp.where(
            jnp.broadcast_to(channel & 127, (width, width)) == lane_id, 1.0, 0.0
        ).astype(BF16)

        def spread(values):
            high, low = split_high_low(values)
            kept = [
                jnp.where(in_group, jnp.broadcast_to(part.astype(F32), (8, width)), 0.0)
                for part in (high, low)
            ]
            return kept

        left = jnp.concatenate(spread(weight) + spread(weight * innovation), axis=0)
        sums = mm_nt(left.astype(BF16), one_hot)
        w_sum = sums[0:8] + sums[8:16]
        b_sum = sums[16:24] + sums[24:32]
        for g in range(groups):
            w_ref[g, pl.ds(slot, 1), :] = w_sum[g : g + 1]
            b_ref[g, pl.ds(slot, 1), :] = b_sum[g : g + 1]

    unroll = 8

    def several(turn, carry):
        for inner in range(unroll):
            one(turn * unroll + inner)
        return carry

    lax.fori_loop(0, slots // unroll, several, 0)


def obs_tables(obs, channels):
    slots, _, width = obs.shape
    shape = jax.ShapeDtypeStruct((channels // width, slots, width), F32)
    return pl.pallas_call(
        obs_tables_kernel,
        out_shape=(shape, shape),
        compiler_params=params(),
        cost_estimate=cost(2 * 32 * slots * width * width, 10 * slots * channels),
        name="obs_tables",
    )(obs)


def observe_kernel(parts_ref, slots_ref, jac_ref, w_ref, b_ref, adj_ref, model_ref):
    count, state, width = parts_ref.shape
    groups = w_ref.shape[0]
    total = parts_ref[0].astype(F32)
    for p in range(1, count):
        total = total + parts_ref[p].astype(F32)
    increment = total.astype(BF16)
    slots = slots_ref.shape[1]
    column_id = lax.broadcasted_iota(I32, (width, slots), 0)
    hits = jnp.where(column_id == jnp.broadcast_to(slots_ref[...], (width, slots)), 1.0, 0.0)
    hits = hits.astype(BF16)
    carried = mm(increment, hits).T.astype(BF16)
    column_adjoint = jnp.zeros((slots, state), F32)
    for g in range(groups):
        jac = jac_ref[g * width : (g + 1) * width, :]
        model = mm_nt(carried, jac)
        model_ref[g] = model
        channel_adjoint = (model * w_ref[g] - b_ref[g]).astype(BF16)
        column_adjoint = column_adjoint + mm(channel_adjoint, jac)
    rounded = column_adjoint.T.astype(BF16)
    adj_ref[...] = mm_nt(rounded, hits).astype(BF16)


def observe(parts, slots, jacobian, w_table, b_table):
    count, state, width = parts.shape
    channels = jacobian.shape[0]
    rows = slots.shape[1]
    return pl.pallas_call(
        observe_kernel,
        out_shape=(
            jax.ShapeDtypeStruct((state, width), BF16),
            jax.ShapeDtypeStruct((channels // width, rows, width), F32),
        ),
        compiler_params=params(),
        cost_estimate=cost(4 * rows * state * channels, 12 * rows * channels),
        name="observe",
    )(parts, slots, jacobian, w_table, b_table)


def pick_kernel(model_ref, obs_ref, o_ref):
    channel = obs_ref[:, 0, :].astype(I32)
    group, lane = channel >> 7, channel & 127
    picked = jnp.zeros(channel.shape, F32)
    for g in range(model_ref.shape[0]):
        taken = jnp.take_along_axis(model_ref[g], lane, axis=1)
        picked = jnp.where(group == g, taken, picked)
    o_ref[...] = picked


def pick(model, obs):
    groups, slots, width = model.shape
    return pl.pallas_call(
        pick_kernel,
        out_shape=jax.ShapeDtypeStruct((slots, width), F32),
        compiler_params=params(),
        cost_estimate=cost(slots * width * 16, 8 * groups * slots * width),
        name="pick",
    )(model, obs)


def member_adjoint_kernel(scale, ens_ref, adj_ref, full_ref, low_ref, high_ref):
    variables = ens_ref.shape[1]
    blocks, width = adj_ref.shape[0], adj_ref.shape[3]
    half_blocks = blocks // 2
    for m in range(ens_ref.shape[0]):
        for k in range(blocks):
            total = None
            for v in range(variables):
                term = ens_ref[m, v, :, k * width : (k + 1) * width].astype(F32) * adj_ref[
                    k, v
                ].astype(F32)
                total = term if total is None else total + term
            total = total * scale
            full_ref[m, :, k * width : (k + 1) * width] = total
            half = low_ref if k < half_blocks else high_ref
            offset = (k % half_blocks) * width
            half[m, :, offset : offset + width] = total.astype(BF16)


def member_adjoint(ensemble, adjoint, scale):
    members, variables, levels, columns = ensemble.shape
    blocks, _, _, width = adjoint.shape
    step = 4
    half = jax.ShapeDtypeStruct((members, levels, HALF), BF16)
    half_spec = pl.BlockSpec((step, levels, HALF), lambda i: (i, 0, 0))
    return pl.pallas_call(
        functools.partial(member_adjoint_kernel, scale),
        out_shape=(jax.ShapeDtypeStruct((members, levels, columns), F32), half, half),
        grid=(members // step,),
        in_specs=[
            pl.BlockSpec((step, variables, levels, columns), lambda i: (i, 0, 0, 0)),
            pl.BlockSpec((blocks, variables, levels, width), lambda i: (0, 0, 0, 0)),
        ],
        out_specs=(
            pl.BlockSpec((step, levels, columns), lambda i: (i, 0, 0)),
            half_spec,
            half_spec,
        ),
        compiler_params=params(),
        cost_estimate=cost(2 * ensemble.size, 4 * ensemble.size),
        name="member_adjoint",
    )(ensemble, adjoint)


def add_halo_kernel(own_ref, low_ref, high_ref, t_after, t_before, o_ref):
    def from_halo(halo_ref, t_ref):
        return mm(halo_ref[...], t_ref[0, 0]) + mm(halo_ref[...], t_ref[0, 1])

    o_ref[:, :HALF] = own_ref[:, :HALF] + from_halo(low_ref, t_after)
    o_ref[:, HALF:] = own_ref[:, HALF:] + from_halo(high_ref, t_before)


def add_halo(own, from_low, from_high, matrices):
    rows, columns = own.shape
    step = 256
    return pl.pallas_call(
        add_halo_kernel,
        out_shape=jax.ShapeDtypeStruct((rows, columns), F32),
        grid=(rows // step,),
        in_specs=[
            pl.BlockSpec((step, columns), lambda i: (i, 0)),
            pl.BlockSpec((step, HALF), lambda i: (i, 0)),
            pl.BlockSpec((step, HALF), lambda i: (i, 0)),
            pl.BlockSpec((1, 2, HALF, HALF), lambda i: (3, 0, 0, 0)),
            pl.BlockSpec((1, 2, HALF, HALF), lambda i: (4, 0, 0, 0)),
        ],
        out_specs=pl.BlockSpec((step, columns), lambda i: (i, 0)),
        compiler_params=params(),
        cost_estimate=cost(2 * 2 * rows * columns * HALF, 10 * rows * columns),
        name="add_halo",
    )(own, from_low, from_high, matrices, matrices)


def swap_halos(low_half, high_half):
    count = lax.axis_size("tile")
    forward = [(i, i + 1) for i in range(count - 1)]
    backward = [(i + 1, i) for i in range(count - 1)]
    from_low = lax.ppermute(high_half, "tile", forward)
    from_high = lax.ppermute(low_half, "tile", backward)
    return from_low, from_high


def coded(values, step):
    return jnp.clip(jnp.round(values * (1.0 / step)), -32767.0, 32767.0).astype(I16)


def body(
    control,
    ensemble,
    jacobian,
    send_columns,
    received_counts,
    observed_channel,
    innovation,
    error_weight,
):
    members, levels, columns = control.shape
    variables = ensemble.shape[1]
    state = variables * levels
    groups = lax.axis_size("mem")
    owners = lax.axis_size("tile")
    scale = 1.0 / math.sqrt(members * groups)
    width = columns // groups
    channels = jacobian.shape[0]
    observed = observed_channel.shape[-1]
    slots = send_columns.shape[-1]
    tile_index = lax.axis_index("tile")
    matrices = jnp.asarray(sweep_matrices())
    edges = jnp.stack(
        [jnp.where(tile_index == 0, 0, 1), jnp.where(tile_index == owners - 1, 2, 1)]
    ).astype(I32)

    from_low, from_high = swap_halos(
        coded(control[:, :, :HALF], CONTROL_STEP), coded(control[:, :, HALF:], CONTROL_STEP)
    )

    filled = (
        jnp.arange(slots, dtype=I32)[None, :, None] < received_counts[0][:, None, None]
    )
    packed = jnp.concatenate(
        [
            observed_channel[0].astype(I16),
            coded(innovation[0], INNOVATION_STEP),
            coded(jnp.where(filled, error_weight[0], 0.0), WEIGHT_STEP),
        ],
        axis=-1,
    )
    obs = lax.all_to_all(packed, "tile", split_axis=0, concat_axis=0, tiled=True)
    obs = obs.reshape(owners * slots, 3, observed)

    own = sweep_own(edges, control.reshape(members * levels, columns), matrices)
    parts = member_sum(
        own.reshape(members, levels, columns),
        from_low,
        from_high,
        ensemble,
        matrices,
        scale,
        groups,
    )
    parts = lax.all_to_all(
        parts.reshape(groups, state, width), "mem", split_axis=0, concat_axis=0, tiled=True
    )
    w_table, b_table = obs_tables(obs, channels)
    block_adjoint, model = observe(
        parts, send_columns.reshape(1, owners * slots), jacobian, w_table, b_table
    )
    adjoint = lax.all_to_all(
        jnp.broadcast_to(block_adjoint[None], (groups, state, width)),
        "mem",
        split_axis=0,
        concat_axis=0,
        tiled=True,
    ).reshape(groups, variables, levels, width)

    evolved = pick(model, obs).reshape(owners, slots, observed)
    evolved = lax.all_to_all(evolved, "tile", split_axis=0, concat_axis=0, tiled=True)
    departures = jnp.where(filled, evolved - innovation[0], 0.0)

    full, low_half, high_half = member_adjoint(ensemble, adjoint, scale)
    from_low, from_high = swap_halos(low_half, high_half)
    own = sweep_own(edges, full.reshape(members * levels, columns), matrices)
    gradient = add_halo(
        own,
        from_low.reshape(members * levels, HALF),
        from_high.reshape(members * levels, HALF),
        matrices,
    )
    return gradient.reshape(members, levels, columns), departures[None]


def solution(mesh):
    in_specs = (
        P("mem", None, "tile"),
        P("mem", None, None, "tile"),
        P(),
        P(("tile", "mem"), None, None),
        P(("tile", "mem"), None),
        P(("tile", "mem"), None, None, None),
        P(("tile", "mem"), None, None, None),
        P(("tile", "mem"), None, None, None),
    )
    out_specs = (P("mem", None, "tile"), P(("tile", "mem"), None, None, None))
    return jax.shard_map(body, mesh=mesh, in_specs=in_specs, out_specs=out_specs, check_vma=False)
```

```python
import functools
import math

import jax
import jax.numpy as jnp
import numpy as np
from jax import lax
from jax.experimental import pallas as pl
from jax.experimental.pallas import tpu as pltpu
from jax.sharding import PartitionSpec as P


NY = 64
SWEEPS = 4
DIFFUSION = 0.2
HALF = SWEEPS * NY

CONTROL_STEP = 8.0 / 32704.0
INNOVATION_STEP = 1.5 / 32700.0
WEIGHT_STEP = 10.0 / 32700.0

F32 = jnp.float32
BF16 = jnp.bfloat16
I16 = jnp.int16
I32 = jnp.int32

VMEM = pl.BlockSpec(memory_space=pltpu.VMEM)
HBM = pl.BlockSpec(memory_space=pltpu.HBM)
SMEM = pl.BlockSpec(memory_space=pltpu.SMEM)


def sweep_matrices():
    y_part = (1.0 - 4.0 * DIFFUSION) * np.eye(NY) + DIFFUSION * (
        np.eye(NY, k=1) + np.eye(NY, k=-1)
    )
    powers = [np.linalg.matrix_power(y_part, n) for n in range(SWEEPS + 1)]
    by_distance = [np.zeros((NY, NY)) for _ in range(SWEEPS + 1)]
    for k in range(SWEEPS + 1):
        for ups in range(k + 1):
            distance = 2 * ups - k
            if distance >= 0:
                by_distance[distance] = by_distance[distance] + (
                    math.comb(SWEEPS, k)
                    * DIFFUSION**k
                    * math.comb(k, ups)
                    * powers[SWEEPS - k]
                )

    def block(distance_of, image_of=None):
        full = np.zeros((HALF, HALF))
        for xi in range(SWEEPS):
            for xo in range(SWEEPS):
                piece = np.zeros((NY, NY))
                if distance_of(xi, xo) <= SWEEPS:
                    piece = piece + by_distance[distance_of(xi, xo)]
                if image_of is not None and image_of(xi, xo) <= SWEEPS:
                    piece = piece - by_distance[image_of(xi, xo)]
                full[xi * NY : (xi + 1) * NY, xo * NY : (xo + 1) * NY] = piece
        return full

    last = SWEEPS - 1
    same = lambda xi, xo: abs(xi - xo)
    blocks = [
        block(same, lambda xi, xo: xi + xo + 2),
        block(same),
        block(same, lambda xi, xo: (last - xi) + (last - xo) + 2),
        block(lambda xi, xo: xo + SWEEPS - xi),
        block(lambda xi, xo: xi + SWEEPS - xo),
    ]
    stacked = np.stack(blocks).astype(np.float32)
    high = stacked.astype(jnp.bfloat16)
    low = (stacked - high.astype(np.float32)).astype(jnp.bfloat16)
    return np.stack([high, low], axis=1)


def split_high_low(values):
    high = values.astype(BF16)
    return high, (values - high.astype(F32)).astype(BF16)


def mm(a, b):
    return jnp.dot(a, b, preferred_element_type=F32)


def mm_nt(a, b):
    return lax.dot_general(a, b, (((1,), (1,)), ((), ())), preferred_element_type=F32)


def in_hbm(x):
    return pltpu.with_memory_space_constraint(x, pltpu.HBM)


def params(**extra):
    return pltpu.CompilerParams(vmem_limit_bytes=24 * 1024 * 1024, **extra)


def cost(flops, bytes_accessed):
    return pl.CostEstimate(flops=flops, bytes_accessed=bytes_accessed, transcendentals=0)


def encode_kernel(x_hbm, low_ref, high_ref, x_ref, sems):
    members = x_hbm.shape[0]
    step = 4
    turns = members // step

    def load(turn):
        at = pl.ds(turn * step, step)
        return pltpu.make_async_copy(x_hbm.at[at], x_ref.at[at], sems.at[turn])

    for turn in range(turns):
        load(turn).start()

    def one(turn, carry):
        load(turn).wait()
        at = pl.ds(turn * step, step)
        coded = jnp.round(x_ref[at] * (1.0 / CONTROL_STEP)).astype(I32).astype(I16)
        low_ref[at] = coded[:, :, :HALF]
        high_ref[at] = coded[:, :, HALF:]
        return carry

    lax.fori_loop(0, turns, one, 0)


def encode(control):
    members, levels, _ = control.shape
    half = jax.ShapeDtypeStruct((members, levels, HALF), I16)
    return pl.pallas_call(
        encode_kernel,
        out_shape=(half, half),
        in_specs=[HBM],
        out_specs=(VMEM, VMEM),
        scratch_shapes=[
            pltpu.VMEM(control.shape, F32),
            pltpu.SemaphoreType.DMA((members // 4,)),
        ],
        compiler_params=params(),
        cost_estimate=cost(4 * control.size, 6 * control.size),
        name="encode",
    )(in_hbm(control))


def pack_kernel(count_ref, channel_ref, innovation_ref, weight_ref, o_ref):
    owners, slots, observed = channel_ref.shape
    slot_id = lax.broadcasted_iota(I32, (slots, observed), 0)
    for s in range(owners):
        filled = slot_id < count_ref[0, s]
        weight = jnp.where(filled, weight_ref[s] * (1.0 / WEIGHT_STEP), 0.0)
        innovation = innovation_ref[s] * (1.0 / INNOVATION_STEP)
        row = [channel_ref[s], jnp.round(innovation).astype(I32), jnp.round(weight).astype(I32)]
        for n, values in enumerate(row):
            o_ref[s, :, n * observed : (n + 1) * observed] = values.astype(I16)


def pack(counts, channel, innovation, weight):
    owners, slots, observed = channel.shape
    return pl.pallas_call(
        pack_kernel,
        out_shape=jax.ShapeDtypeStruct((owners, slots, 3 * observed), I16),
        in_specs=[SMEM, VMEM, VMEM, VMEM],
        out_specs=VMEM,
        compiler_params=params(),
        cost_estimate=cost(10 * channel.size, 18 * channel.size),
        name="pack",
    )(counts, channel, innovation, weight)


def depart_kernel(count_ref, evolved_ref, innovation_ref, o_ref):
    owners, slots, observed = evolved_ref.shape
    slot_id = lax.broadcasted_iota(I32, (slots, observed), 0)
    for s in range(owners):
        filled = slot_id < count_ref[0, s]
        o_ref[s] = jnp.where(filled, evolved_ref[s] - innovation_ref[s], 0.0)


def depart(counts, evolved, innovation):
    return pl.pallas_call(
        depart_kernel,
        out_shape=jax.ShapeDtypeStruct(evolved.shape, F32),
        in_specs=[SMEM, VMEM, VMEM],
        out_specs=VMEM,
        compiler_params=params(),
        cost_estimate=cost(2 * evolved.size, 12 * evolved.size),
        name="depart",
    )(counts, evolved, innovation)


def sweep_rows(edge_ref, x_ref, t_ref, o_ref, step, ready):
    def apply(high, low, index):
        t_high, t_low = t_ref[index, 0], t_ref[index, 1]
        return mm(high, t_high) + mm(low, t_high) + mm(high, t_low)

    def one(turn, carry):
        ready(turn)
        at = pl.ds(pl.multiple_of(turn * step, step), step)
        left_high, left_low = split_high_low(x_ref[at, :HALF])
        right_high, right_low = split_high_low(x_ref[at, HALF:])
        o_ref[at, :HALF] = apply(left_high, left_low, edge_ref[0]) + apply(
            right_high, right_low, 4
        )
        o_ref[at, HALF:] = apply(right_high, right_low, edge_ref[1]) + apply(
            left_high, left_low, 3
        )
        return carry

    lax.fori_loop(0, x_ref.shape[0] // step, one, 0)


def sweep_near_kernel(edge_ref, x_ref, t_ref, o_ref):
    sweep_rows(edge_ref, x_ref, t_ref, o_ref, 256, lambda turn: None)


def sweep_far_kernel(edge_ref, x_hbm, t_ref, o_ref, x_ref, sems):
    rows = x_hbm.shape[0]
    step = 256

    def load(turn):
        at = pl.ds(turn * step, step)
        return pltpu.make_async_copy(x_hbm.at[at], x_ref.at[at], sems.at[turn])

    for turn in range(rows // step):
        load(turn).start()
    sweep_rows(edge_ref, x_ref, t_ref, o_ref, step, lambda turn: load(turn).wait())


def sweep_own(edges, field, matrices, far):
    rows, columns = field.shape
    scratch = [pltpu.VMEM(field.shape, F32), pltpu.SemaphoreType.DMA((rows // 256,))]
    return pl.pallas_call(
        sweep_far_kernel if far else sweep_near_kernel,
        out_shape=jax.ShapeDtypeStruct((rows, columns), F32),
        in_specs=[SMEM, HBM if far else VMEM, VMEM],
        out_specs=VMEM,
        scratch_shapes=scratch if far else [],
        compiler_params=params(),
        cost_estimate=cost(2 * 6 * rows * columns * HALF, 10 * rows * columns),
        name="sweep_own",
    )(edges, in_hbm(field) if far else field, matrices)


LEVEL_STEP = 16


def level_copies(source, target, sems):
    def copy(turn):
        at = pl.ds(turn * LEVEL_STEP, LEVEL_STEP)
        return pltpu.make_async_copy(
            source.at[:, :, at, :], target.at[:, :, at, :], sems.at[turn]
        )

    return copy


def member_sum_kernel(
    scale, own_ref, low_ref, high_ref, ens_hbm, t_ref, o_hbm, ens_ref, o_ref, in_sems, out_sems
):
    members, variables, levels, _ = ens_ref.shape
    blocks, width = o_ref.shape[0], o_ref.shape[3]
    half_blocks = blocks // 2
    step = LEVEL_STEP
    load = level_copies(ens_hbm, ens_ref, in_sems)
    save = level_copies(o_ref, o_hbm, out_sems)
    for turn in range(levels // step):
        load(turn).start()

    def one(turn, carry):
        at = pl.ds(pl.multiple_of(turn * step, step), step)

        def from_halo(halo_ref, index):
            coded = halo_ref[:, at, :].astype(I32).reshape(members * step, HALF)
            upper = (coded >> 8).astype(F32).astype(BF16)
            lower = (coded & 255).astype(F32).astype(BF16)
            upper_part = mm(upper, t_ref[index, 0]) + mm(upper, t_ref[index, 1])
            lower_part = mm(lower, t_ref[index, 0])
            total = (upper_part * 256.0 + lower_part) * CONTROL_STEP
            return total.reshape(members, step, HALF)

        halos = [from_halo(low_ref, 3), from_halo(high_ref, 4)]
        load(turn).wait()
        for k in range(blocks):
            offset = (k % half_blocks) * width
            halo = halos[k // half_blocks][:, :, offset : offset + width]
            weights = own_ref[:, at, k * width : (k + 1) * width] + halo
            weights = weights.astype(BF16).astype(F32)
            for v in range(variables):
                total = None
                for m in range(members):
                    term = weights[m] * ens_ref[m, v, at, k * width : (k + 1) * width].astype(F32)
                    total = term if total is None else total + term
                o_ref[k, v, at, :] = (total * scale).astype(BF16)
        save(turn).start()
        return carry

    lax.fori_loop(0, levels // step, one, 0)
    for turn in range(levels // step):
        save(turn).wait()


def member_sum(own, from_low, from_high, ensemble, matrices, scale, blocks):
    members, variables, levels, columns = ensemble.shape
    width = columns // blocks
    turns = levels // LEVEL_STEP
    shape = (blocks, variables, levels, width)
    return pl.pallas_call(
        functools.partial(member_sum_kernel, scale),
        out_shape=pltpu.HBM(shape, BF16),
        in_specs=[VMEM, VMEM, VMEM, HBM, VMEM],
        out_specs=HBM,
        scratch_shapes=[
            pltpu.VMEM(ensemble.shape, BF16),
            pltpu.VMEM(shape, BF16),
            pltpu.SemaphoreType.DMA((turns,)),
            pltpu.SemaphoreType.DMA((turns,)),
        ],
        compiler_params=params(),
        cost_estimate=cost(
            2 * 3 * members * levels * columns * HALF, 2 * ensemble.size + 6 * own.size
        ),
        name="member_sum",
    )(own, from_low, from_high, in_hbm(ensemble), matrices)


def obs_tables_kernel(obs_ref, w_ref, b_ref, channel_ref):
    owners, slots, _ = obs_ref.shape
    groups, _, width = w_ref.shape
    group_id = lax.broadcasted_iota(I32, (8, width), 0)
    lane_id = lax.broadcasted_iota(I32, (width, width), 0)

    def one(owner, slot):
        row = obs_ref[owner].astype(I32)[slot : slot + 1]
        channel = row[:, :width]
        innovation = row[:, width : 2 * width].astype(F32) * INNOVATION_STEP
        weight = row[:, 2 * width :].astype(F32) * WEIGHT_STEP
        in_group = jnp.broadcast_to(channel >> 7, (8, width)) == group_id
        one_hot = jnp.where(
            jnp.broadcast_to(channel & 127, (width, width)) == lane_id, 1.0, 0.0
        ).astype(BF16)

        def spread(values):
            return [
                jnp.where(in_group, jnp.broadcast_to(part.astype(F32), (8, width)), 0.0)
                for part in split_high_low(values)
            ]

        left = jnp.concatenate(spread(weight) + spread(weight * innovation), axis=0)
        sums = mm_nt(left.astype(BF16), one_hot)
        w_sum = sums[0:8] + sums[8:16]
        b_sum = sums[16:24] + sums[24:32]
        at = pl.ds(owner * slots + slot, 1)
        channel_ref[at, :] = channel
        for g in range(groups):
            w_ref[g, at, :] = w_sum[g : g + 1]
            b_ref[g, at, :] = b_sum[g : g + 1]

    unroll = 4

    def several(turn, carry):
        for inner in range(unroll):
            for slot in range(slots):
                one(turn * unroll + inner, slot)
        return carry

    lax.fori_loop(0, owners // unroll, several, 0)


def obs_tables(obs, channels):
    owners, slots, packed = obs.shape
    width = packed // 3
    rows = owners * slots
    shape = jax.ShapeDtypeStruct((channels // width, rows, width), F32)
    return pl.pallas_call(
        obs_tables_kernel,
        out_shape=(shape, shape, jax.ShapeDtypeStruct((rows, width), I32)),
        compiler_params=params(),
        cost_estimate=cost(2 * 32 * rows * width * width, 10 * rows * channels),
        name="obs_tables",
    )(obs)


def observe_kernel(
    parts_ref, slots_ref, jac_ref, w_ref, b_ref, adj_hbm, model_ref, adj_ref, sems
):
    count, state, width = parts_ref.shape
    groups = w_ref.shape[0]
    total = parts_ref[0].astype(F32)
    for p in range(1, count):
        total = total + parts_ref[p].astype(F32)
    increment = total.astype(BF16)
    slots = slots_ref.shape[1]
    column_id = lax.broadcasted_iota(I32, (width, slots), 0)
    hits = jnp.where(column_id == jnp.broadcast_to(slots_ref[...], (width, slots)), 1.0, 0.0)
    hits = hits.astype(BF16)
    carried = mm(increment, hits).T.astype(BF16)
    column_adjoint = jnp.zeros((slots, state), F32)
    for g in range(groups):
        jac = jac_ref[g * width : (g + 1) * width, :]
        model = mm_nt(carried, jac)
        model_ref[g] = model
        channel_adjoint = (model * w_ref[g] - b_ref[g]).astype(BF16)
        column_adjoint = column_adjoint + mm(channel_adjoint, jac)
    rounded = column_adjoint.T.astype(BF16)
    adj_ref[...] = mm_nt(rounded, hits).astype(BF16)
    copies = [
        pltpu.make_async_copy(adj_ref, adj_hbm.at[p], sems.at[p]) for p in range(count)
    ]
    for copy in copies:
        copy.start()
    for copy in copies:
        copy.wait()


def observe(parts, slots, jacobian, w_table, b_table):
    count, state, width = parts.shape
    channels = jacobian.shape[0]
    rows = slots.shape[1]
    return pl.pallas_call(
        observe_kernel,
        out_shape=(
            pltpu.HBM((count, state, width), BF16),
            jax.ShapeDtypeStruct((channels // width, rows, width), F32),
        ),
        in_specs=[VMEM] * 5,
        out_specs=(HBM, VMEM),
        scratch_shapes=[
            pltpu.VMEM((state, width), BF16),
            pltpu.SemaphoreType.DMA((count,)),
        ],
        compiler_params=params(),
        cost_estimate=cost(4 * rows * state * channels, 12 * rows * channels),
        name="observe",
    )(parts, slots, jacobian, w_table, b_table)


def pick_kernel(model_ref, channel_ref, o_hbm, o_ref, sem):
    channel = channel_ref[...]
    group, lane = channel >> 7, channel & 127
    picked = jnp.zeros(channel.shape, F32)
    for g in range(model_ref.shape[0]):
        taken = jnp.take_along_axis(model_ref[g], lane, axis=1)
        picked = jnp.where(group == g, taken, picked)
    o_ref[...] = picked
    copy = pltpu.make_async_copy(o_ref, o_hbm, sem)
    copy.start()
    copy.wait()


def pick(model, channel):
    groups, slots, width = model.shape
    return pl.pallas_call(
        pick_kernel,
        out_shape=pltpu.HBM((slots, width), F32),
        in_specs=[VMEM, VMEM],
        out_specs=HBM,
        scratch_shapes=[pltpu.VMEM((slots, width), F32), pltpu.SemaphoreType.DMA],
        compiler_params=params(),
        cost_estimate=cost(slots * width * 16, 8 * groups * slots * width),
        name="pick",
    )(model, channel)


def member_adjoint_kernel(
    scale, ens_hbm, adj_ref, full_hbm, low_ref, high_ref, ens_ref, full_ref, sems, out_sems
):
    members, variables, levels, _ = ens_ref.shape
    blocks, width = adj_ref.shape[0], adj_ref.shape[3]
    half_blocks = blocks // 2
    step = LEVEL_STEP
    load = level_copies(ens_hbm, ens_ref, sems)
    for turn in range(levels // step):
        load(turn).start()

    def save(turn):
        at = pl.ds(turn * step, step)
        return pltpu.make_async_copy(
            full_ref.at[:, at, :], full_hbm.at[:, at, :], out_sems.at[turn]
        )

    def one(turn, carry):
        at = pl.ds(pl.multiple_of(turn * step, step), step)
        load(turn).wait()
        for k in range(blocks):
            adjoint = [adj_ref[k, v, at, :].astype(F32) * scale for v in range(variables)]
            half = low_ref if k < half_blocks else high_ref
            offset = (k % half_blocks) * width
            for m in range(members):
                total = None
                for v in range(variables):
                    term = ens_ref[m, v, at, k * width : (k + 1) * width].astype(F32) * adjoint[v]
                    total = term if total is None else total + term
                full_ref[m, at, k * width : (k + 1) * width] = total
                half[m, at, offset : offset + width] = total.astype(BF16)
        save(turn).start()
        return carry

    lax.fori_loop(0, levels // step, one, 0)
    for turn in range(levels // step):
        save(turn).wait()


def member_adjoint(ensemble, adjoint, scale):
    members, _, levels, columns = ensemble.shape
    half = jax.ShapeDtypeStruct((members, levels, HALF), BF16)
    return pl.pallas_call(
        functools.partial(member_adjoint_kernel, scale),
        out_shape=(pltpu.HBM((members, levels, columns), F32), half, half),
        in_specs=[HBM, VMEM],
        out_specs=(HBM, VMEM, VMEM),
        scratch_shapes=[
            pltpu.VMEM(ensemble.shape, BF16),
            pltpu.VMEM((members, levels, columns), F32),
            pltpu.SemaphoreType.DMA((levels // LEVEL_STEP,)),
            pltpu.SemaphoreType.DMA((levels // LEVEL_STEP,)),
        ],
        compiler_params=params(),
        cost_estimate=cost(2 * ensemble.size, 4 * ensemble.size),
        name="member_adjoint",
    )(in_hbm(ensemble), adjoint)


def add_halo_kernel(own_ref, low_ref, high_ref, t_ref, o_ref):
    i = pl.program_id(0)
    step = o_ref.shape[0]
    at = pl.ds(pl.multiple_of(i * step, step), step)

    def from_halo(halo_ref, index):
        halo = halo_ref[at, :]
        return mm(halo, t_ref[index, 0]) + mm(halo, t_ref[index, 1])

    o_ref[:, :HALF] = own_ref[at, :HALF] + from_halo(low_ref, 3)
    o_ref[:, HALF:] = own_ref[at, HALF:] + from_halo(high_ref, 4)


def add_halo(own, from_low, from_high, matrices):
    rows, columns = own.shape
    step = 256
    return pl.pallas_call(
        add_halo_kernel,
        out_shape=jax.ShapeDtypeStruct((rows, columns), F32),
        grid=(rows // step,),
        in_specs=[VMEM] * 4,
        out_specs=pl.BlockSpec((step, columns), lambda i: (i, 0)),
        compiler_params=params(),
        cost_estimate=cost(2 * 2 * rows * columns * HALF, 10 * rows * columns),
        name="add_halo",
    )(own, from_low, from_high, matrices)


def swap_halos(low_half, high_half):
    count = lax.axis_size("tile")
    forward = [(i, i + 1) for i in range(count - 1)]
    backward = [(i + 1, i) for i in range(count - 1)]
    from_low = lax.ppermute(high_half, "tile", forward)
    from_high = lax.ppermute(low_half, "tile", backward)
    return from_low, from_high


def body(
    control,
    ensemble,
    jacobian,
    send_columns,
    received_counts,
    observed_channel,
    innovation,
    error_weight,
):
    members, levels, columns = control.shape
    variables = ensemble.shape[1]
    state = variables * levels
    groups = lax.axis_size("mem")
    owners = lax.axis_size("tile")
    scale = 1.0 / math.sqrt(members * groups)
    width = columns // groups
    channels = jacobian.shape[0]
    observed = observed_channel.shape[-1]
    slots = send_columns.shape[-1]
    tile_index = lax.axis_index("tile")
    matrices = jnp.asarray(sweep_matrices())
    edges = jnp.stack(
        [jnp.where(tile_index == 0, 0, 1), jnp.where(tile_index == owners - 1, 2, 1)]
    ).astype(I32)

    counts = received_counts
    from_low, from_high = swap_halos(*encode(control))
    own = sweep_own(edges, control.reshape(members * levels, columns), matrices, True)
    packed = pack(counts, observed_channel[0], innovation[0], error_weight[0])
    packed, own = lax.optimization_barrier((packed, own))
    obs = lax.all_to_all(packed, "tile", split_axis=0, concat_axis=0, tiled=True)
    parts = member_sum(
        own.reshape(members, levels, columns),
        from_low,
        from_high,
        ensemble,
        matrices,
        scale,
        groups,
    )
    parts = lax.all_to_all(
        parts.reshape(groups, state, width), "mem", split_axis=0, concat_axis=0, tiled=True
    )
    w_table, b_table, channel = obs_tables(obs, channels)
    block_adjoint, model = observe(
        parts, send_columns.reshape(1, owners * slots), jacobian, w_table, b_table
    )
    adjoint = lax.all_to_all(
        block_adjoint, "mem", split_axis=0, concat_axis=0, tiled=True
    ).reshape(groups, variables, levels, width)
    evolved = pick(model, channel).reshape(owners, slots, observed)
    evolved = lax.all_to_all(evolved, "tile", split_axis=0, concat_axis=0, tiled=True)
    full, low_half, high_half = member_adjoint(ensemble, adjoint, scale)
    from_low, from_high = swap_halos(low_half, high_half)
    own = sweep_own(edges, full.reshape(members * levels, columns), matrices, True)
    departures = depart(counts, evolved, innovation[0])
    gradient = add_halo(
        own,
        from_low.reshape(members * levels, HALF),
        from_high.reshape(members * levels, HALF),
        matrices,
    )
    return gradient.reshape(members, levels, columns), departures[None]


def solution(mesh):
    in_specs = (
        P("mem", None, "tile"),
        P("mem", None, None, "tile"),
        P(),
        P(("tile", "mem"), None, None),
        P(("tile", "mem"), None),
        P(("tile", "mem"), None, None, None),
        P(("tile", "mem"), None, None, None),
        P(("tile", "mem"), None, None, None),
    )
    out_specs = (P("mem", None, "tile"), P(("tile", "mem"), None, None, None))
    return jax.shard_map(body, mesh=mesh, in_specs=in_specs, out_specs=out_specs, check_vma=False)
```

```python
import functools
import math

import jax
import jax.numpy as jnp
import numpy as np
from jax import lax
from jax.experimental import pallas as pl
from jax.experimental.pallas import tpu as pltpu
from jax.sharding import PartitionSpec as P


NY = 64
SWEEPS = 4
SWEEP_SCALE = 0.2**SWEEPS
HALF = SWEEPS * NY

CONTROL_STEP = 8.0 / 32704.0
INNOVATION_STEP = 1.5 / 32700.0
WEIGHT_STEP = 10.0 / 32700.0

F32 = jnp.float32
BF16 = jnp.bfloat16
I16 = jnp.int16
I32 = jnp.int32

VMEM = pl.BlockSpec(memory_space=pltpu.VMEM)
HBM = pl.BlockSpec(memory_space=pltpu.HBM)
SMEM = pl.BlockSpec(memory_space=pltpu.SMEM)


def sweep_matrices():
    y_part = np.eye(NY) + np.eye(NY, k=1) + np.eye(NY, k=-1)
    powers = [np.linalg.matrix_power(y_part, n) for n in range(SWEEPS + 1)]
    by_distance = [np.zeros((NY, NY)) for _ in range(SWEEPS + 1)]
    for k in range(SWEEPS + 1):
        for ups in range(k + 1):
            distance = 2 * ups - k
            if distance >= 0:
                by_distance[distance] = (
                    by_distance[distance]
                    + math.comb(SWEEPS, k) * math.comb(k, ups) * powers[SWEEPS - k]
                )

    def block(distance_of, image_of=None):
        full = np.zeros((HALF, HALF))
        for xi in range(SWEEPS):
            for xo in range(SWEEPS):
                piece = np.zeros((NY, NY))
                if distance_of(xi, xo) <= SWEEPS:
                    piece = piece + by_distance[distance_of(xi, xo)]
                if image_of is not None and image_of(xi, xo) <= SWEEPS:
                    piece = piece - by_distance[image_of(xi, xo)]
                full[xi * NY : (xi + 1) * NY, xo * NY : (xo + 1) * NY] = piece
        return full

    last = SWEEPS - 1
    same = lambda xi, xo: abs(xi - xo)
    blocks = [
        block(same, lambda xi, xo: xi + xo + 2),
        block(same),
        block(same, lambda xi, xo: (last - xi) + (last - xo) + 2),
        block(lambda xi, xo: xo + SWEEPS - xi),
        block(lambda xi, xo: xi + SWEEPS - xo),
    ]
    return np.stack(blocks).astype(jnp.bfloat16)


def split_high_low(values):
    high = values.astype(BF16)
    return high, (values - high.astype(F32)).astype(BF16)


def mm(a, b):
    return jnp.dot(a, b, preferred_element_type=F32)


def mm_nt(a, b):
    return lax.dot_general(a, b, (((1,), (1,)), ((), ())), preferred_element_type=F32)


def in_vmem(x):
    return pltpu.with_memory_space_constraint(x, pltpu.VMEM)


def in_hbm(x):
    return pltpu.with_memory_space_constraint(x, pltpu.HBM)


def params(**extra):
    return pltpu.CompilerParams(vmem_limit_bytes=24 * 1024 * 1024, **extra)


def cost(flops, bytes_accessed):
    return pl.CostEstimate(flops=flops, bytes_accessed=bytes_accessed, transcendentals=0)


ENCODE_STEP = 4


def encode_kernel(
    count_ref,
    x_hbm,
    channel_hbm,
    innovation_hbm,
    weight_hbm,
    low_hbm,
    high_hbm,
    packed_hbm,
    x_ref,
    channel_ref,
    innovation_ref,
    weight_ref,
    low_ref,
    high_ref,
    packed_ref,
    in_sems,
    obs_sems,
    low_sems,
    high_sems,
    packed_sem,
):
    turns = x_hbm.shape[0] // ENCODE_STEP
    owners, slots, observed = channel_hbm.shape

    def chunk(source, target, sems, turn):
        at = pl.ds(turn * ENCODE_STEP, ENCODE_STEP)
        return pltpu.make_async_copy(source.at[at], target.at[at], sems.at[turn])

    obs_loads = [
        pltpu.make_async_copy(channel_hbm, channel_ref, obs_sems.at[0]),
        pltpu.make_async_copy(innovation_hbm, innovation_ref, obs_sems.at[1]),
        pltpu.make_async_copy(weight_hbm, weight_ref, obs_sems.at[2]),
    ]
    for turn in range(turns - 1):
        chunk(x_hbm, x_ref, in_sems, turn).start()
    for copy in obs_loads:
        copy.start()
    chunk(x_hbm, x_ref, in_sems, turns - 1).start()
    saves = []

    def encode_chunk(turn):
        chunk(x_hbm, x_ref, in_sems, turn).wait()
        at = slice(turn * ENCODE_STEP, (turn + 1) * ENCODE_STEP)
        coded = jnp.round(x_ref[at] * (1.0 / CONTROL_STEP)).astype(I32).astype(I16)
        low_ref[at] = coded[:, :, :HALF]
        high_ref[at] = coded[:, :, HALF:]
        for source, target, sems in (
            (low_ref, low_hbm, low_sems),
            (high_ref, high_hbm, high_sems),
        ):
            saves.append(chunk(source, target, sems, turn))
            saves[-1].start()

    for turn in range(turns - 1):
        encode_chunk(turn)
    for copy in obs_loads:
        copy.wait()
    slot_id = lax.broadcasted_iota(I32, (slots, observed), 0)
    for s in range(owners):
        filled = slot_id < count_ref[0, s]
        weight = jnp.where(filled, weight_ref[s] * (1.0 / WEIGHT_STEP), 0.0)
        innovation = innovation_ref[s] * (1.0 / INNOVATION_STEP)
        row = [channel_ref[s], jnp.round(innovation).astype(I32), jnp.round(weight).astype(I32)]
        for n, values in enumerate(row):
            packed_ref[s, :, n * observed : (n + 1) * observed] = values.astype(I16)
    saves.append(pltpu.make_async_copy(packed_ref, packed_hbm, packed_sem))
    saves[-1].start()
    encode_chunk(turns - 1)
    for copy in saves:
        copy.wait()


def encode(counts, control, channel, innovation, weight):
    members, levels, _ = control.shape
    owners, slots, observed = channel.shape
    turns = members // ENCODE_STEP
    half = (members, levels, HALF)
    packed = (owners, slots, 3 * observed)
    return pl.pallas_call(
        encode_kernel,
        out_shape=(pltpu.HBM(half, I16), pltpu.HBM(half, I16), pltpu.HBM(packed, I16)),
        in_specs=[SMEM, HBM, HBM, HBM, HBM],
        out_specs=(HBM, HBM, HBM),
        scratch_shapes=[
            pltpu.VMEM(control.shape, F32),
            pltpu.VMEM(channel.shape, I32),
            pltpu.VMEM(channel.shape, F32),
            pltpu.VMEM(channel.shape, F32),
            pltpu.VMEM(half, I16),
            pltpu.VMEM(half, I16),
            pltpu.VMEM(packed, I16),
            pltpu.SemaphoreType.DMA((turns,)),
            pltpu.SemaphoreType.DMA((3,)),
            pltpu.SemaphoreType.DMA((turns,)),
            pltpu.SemaphoreType.DMA((turns,)),
            pltpu.SemaphoreType.DMA,
        ],
        compiler_params=params(),
        cost_estimate=cost(4 * control.size, 6 * control.size),
        name="encode",
    )(counts, *[in_hbm(x) for x in (control, channel, innovation, weight)])


def depart_kernel(count_ref, evolved_ref, innovation_ref, o_ref):
    owners, slots, observed = evolved_ref.shape
    slot_id = lax.broadcasted_iota(I32, (slots, observed), 0)
    for s in range(owners):
        filled = slot_id < count_ref[0, s]
        o_ref[s] = jnp.where(filled, evolved_ref[s], 0.0) - innovation_ref[s]


def depart(counts, evolved, innovation):
    return pl.pallas_call(
        depart_kernel,
        out_shape=jax.ShapeDtypeStruct(evolved.shape, F32),
        in_specs=[SMEM, VMEM, VMEM],
        out_specs=VMEM,
        compiler_params=params(),
        cost_estimate=cost(2 * evolved.size, 12 * evolved.size),
        name="depart",
    )(counts, evolved, innovation)


def sweep_rows(edge_ref, x_ref, t_ref, o_ref, step, ready):
    def apply(high, low, index):
        return mm(high, t_ref[index]) + mm(low, t_ref[index])

    def one(turn, carry):
        ready(turn)
        at = pl.ds(pl.multiple_of(turn * step, step), step)
        left_high, left_low = split_high_low(x_ref[at, :HALF] * SWEEP_SCALE)
        right_high, right_low = split_high_low(x_ref[at, HALF:] * SWEEP_SCALE)
        o_ref[at, :HALF] = apply(left_high, left_low, edge_ref[0]) + apply(
            right_high, right_low, 4
        )
        o_ref[at, HALF:] = apply(right_high, right_low, edge_ref[1]) + apply(
            left_high, left_low, 3
        )
        return carry

    lax.fori_loop(0, x_ref.shape[0] // step, one, 0)


def sweep_near_kernel(edge_ref, x_ref, t_ref, o_ref):
    sweep_rows(edge_ref, x_ref, t_ref, o_ref, 256, lambda turn: None)


def sweep_far_kernel(edge_ref, x_hbm, t_ref, o_ref, x_ref, sems):
    rows = x_hbm.shape[0]
    step = 256

    def load(turn):
        at = pl.ds(turn * step, step)
        return pltpu.make_async_copy(x_hbm.at[at], x_ref.at[at], sems.at[turn])

    for turn in range(rows // step):
        load(turn).start()
    sweep_rows(edge_ref, x_ref, t_ref, o_ref, step, lambda turn: load(turn).wait())


def sweep_own(edges, field, matrices, far):
    rows, columns = field.shape
    scratch = [pltpu.VMEM(field.shape, F32), pltpu.SemaphoreType.DMA((rows // 256,))]
    return pl.pallas_call(
        sweep_far_kernel if far else sweep_near_kernel,
        out_shape=jax.ShapeDtypeStruct((rows, columns), F32),
        in_specs=[SMEM, HBM if far else VMEM, VMEM],
        out_specs=VMEM,
        scratch_shapes=scratch if far else [],
        compiler_params=params(),
        cost_estimate=cost(2 * 6 * rows * columns * HALF, 10 * rows * columns),
        name="sweep_own",
    )(edges, in_hbm(field) if far else field, matrices)


LEVEL_STEP = 16


def level_copies(source, target, sems):
    def copy(turn):
        at = pl.ds(turn * LEVEL_STEP, LEVEL_STEP)
        return pltpu.make_async_copy(
            source.at[:, :, at, :], target.at[:, :, at, :], sems.at[turn]
        )

    return copy


def localize_sum_kernel(
    scale,
    place_ref,
    x_ref,
    low_ref,
    high_ref,
    ens_hbm,
    t_hbm,
    own_hbm,
    one_hbm,
    two_hbm,
    three_hbm,
    ens_ref,
    t_ref,
    w_even,
    w_odd,
    o_ref,
    in_sems,
    t_sem,
    out_sems,
):
    members, variables, levels, _ = ens_ref.shape
    blocks, width = o_ref.shape[0], o_ref.shape[3]
    step = LEVEL_STEP
    turns = levels // step
    load = level_copies(ens_hbm, ens_ref, in_sems)
    t_load = pltpu.make_async_copy(t_hbm, t_ref, t_sem)
    t_load.start()
    for turn in range(turns):
        load(turn).start()

    def apply(high, low, index):
        return mm(high, t_ref[index]) + mm(low, t_ref[index])

    def weigh(turn, w_ref):
        at = pl.ds(turn * step, step)
        rows = members * step
        left_high, left_low = split_high_low(x_ref[:, at, :HALF].reshape(rows, HALF))
        right_high, right_low = split_high_low(x_ref[:, at, HALF:].reshape(rows, HALF))

        def from_halo(halo_ref, index):
            coded = halo_ref[:, at, :].reshape(rows, HALF).astype(I32)
            upper = (coded >> 8).astype(F32).astype(BF16)
            lower = (coded & 255).astype(F32).astype(BF16)
            return (mm(upper, t_ref[index]) * 256.0 + mm(lower, t_ref[index])) * CONTROL_STEP

        left = (
            apply(left_high, left_low, place_ref[0])
            + apply(right_high, right_low, 4)
            + from_halo(low_ref, 3)
        )
        right = (
            apply(right_high, right_low, place_ref[1])
            + apply(left_high, left_low, 3)
            + from_halo(high_ref, 4)
        )
        left, right = left * SWEEP_SCALE, right * SWEEP_SCALE
        w_ref[:, :, :HALF] = left.astype(BF16).reshape(members, step, HALF)
        w_ref[:, :, HALF:] = right.astype(BF16).reshape(members, step, HALF)

    def total_up(turn, w_ref):
        at = pl.ds(turn * step, step)
        for k in range(blocks):
            across = slice(k * width, (k + 1) * width)
            totals = [None] * variables
            for m in range(members):
                weight = w_ref[m, :, across].astype(F32)
                for v in range(variables):
                    term = weight * ens_ref[m, v, at, across].astype(F32)
                    totals[v] = term if totals[v] is None else totals[v] + term
            for v in range(variables):
                o_ref[k, v, at, :] = (totals[v] * scale).astype(BF16)

    buffers = [w_even, w_odd]
    t_load.wait()
    weigh(0, buffers[0])
    for turn in range(turns):
        load(turn).wait()
        if turn + 1 < turns:
            weigh(turn + 1, buffers[(turn + 1) % 2])
        total_up(turn, buffers[turn % 2])
    mine = place_ref[2]
    copies = [
        pltpu.make_async_copy(o_ref.at[lax.rem(mine + s, blocks)], target, out_sems.at[s])
        for s, target in enumerate((own_hbm, one_hbm, two_hbm, three_hbm))
    ]
    for copy in copies:
        copy.start()
    for copy in copies:
        copy.wait()


def localize_sum(place, control, from_low, from_high, ensemble, matrices, scale, blocks):
    members, variables, levels, columns = ensemble.shape
    width = columns // blocks
    turns = levels // LEVEL_STEP
    piece = pltpu.HBM((variables, levels, width), BF16)
    return pl.pallas_call(
        functools.partial(localize_sum_kernel, scale),
        out_shape=(piece,) * blocks,
        in_specs=[SMEM, VMEM, VMEM, VMEM, HBM, HBM],
        out_specs=(HBM,) * blocks,
        scratch_shapes=[
            pltpu.VMEM(ensemble.shape, BF16),
            pltpu.VMEM(matrices.shape, BF16),
            pltpu.VMEM((members, LEVEL_STEP, columns), BF16),
            pltpu.VMEM((members, LEVEL_STEP, columns), BF16),
            pltpu.VMEM((blocks, variables, levels, width), BF16),
            pltpu.SemaphoreType.DMA((turns,)),
            pltpu.SemaphoreType.DMA,
            pltpu.SemaphoreType.DMA((blocks,)),
        ],
        compiler_params=params(),
        cost_estimate=cost(
            2 * 6 * members * levels * columns * HALF, 2 * ensemble.size + 8 * control.size
        ),
        name="localize_sum",
    )(
        place,
        in_vmem(control),
        in_vmem(from_low),
        in_vmem(from_high),
        in_hbm(ensemble),
        in_hbm(matrices),
    )


def obs_tables_kernel(
    obs_ref, own_hbm, slots_hbm, w_ref, b_ref, channel_ref, own_ref, slots_ref, sems
):
    copies = [
        pltpu.make_async_copy(own_hbm, own_ref, sems.at[0]),
        pltpu.make_async_copy(slots_hbm, slots_ref, sems.at[1]),
    ]
    for copy in copies:
        copy.start()
    owners, slots, _ = obs_ref.shape
    groups, _, width = w_ref.shape
    group_id = lax.broadcasted_iota(I32, (8, width), 0)
    lane_id = lax.broadcasted_iota(I32, (width, width), 0).astype(F32).astype(BF16)
    one_bf, zero_bf = jnp.ones((), BF16), jnp.zeros((), BF16)

    def one(owner, slot):
        row = obs_ref[owner].astype(I32)[slot : slot + 1]
        channel = row[:, :width]
        innovation = row[:, width : 2 * width].astype(F32) * INNOVATION_STEP
        weight = row[:, 2 * width :].astype(F32) * WEIGHT_STEP
        in_group = jnp.broadcast_to(channel >> 7, (8, width)) == group_id
        lane = (channel & 127).astype(F32).astype(BF16)
        one_hot = jnp.where(jnp.broadcast_to(lane, (width, width)) == lane_id, one_bf, zero_bf)

        def spread(values):
            return [
                jnp.where(in_group, jnp.broadcast_to(part.astype(F32), (8, width)), 0.0)
                for part in split_high_low(values)
            ]

        left = jnp.concatenate(spread(weight) + spread(weight * innovation), axis=0)
        sums = mm_nt(left.astype(BF16), one_hot)
        w_sum = sums[0:8] + sums[8:16]
        b_sum = sums[16:24] + sums[24:32]
        at = pl.ds(slot * owners + owner, 1)
        channel_ref[at, :] = channel
        for g in range(groups):
            w_ref[g, at, :] = w_sum[g : g + 1]
            b_ref[g, at, :] = b_sum[g : g + 1]

    unroll = 4

    def several(turn, carry):
        for inner in range(unroll):
            for slot in range(slots):
                one(turn * unroll + inner, slot)
        return carry

    lax.fori_loop(0, owners // unroll, several, 0)
    for copy in copies:
        copy.wait()


def obs_tables(obs, own, columns, channels):
    owners, slots, packed = obs.shape
    width = packed // 3
    rows = owners * slots
    shape = jax.ShapeDtypeStruct((channels // width, rows, width), F32)
    return pl.pallas_call(
        obs_tables_kernel,
        out_shape=(
            shape,
            shape,
            jax.ShapeDtypeStruct((rows, width), I32),
            jax.ShapeDtypeStruct(own.shape, own.dtype),
            jax.ShapeDtypeStruct(columns.shape, columns.dtype),
        ),
        in_specs=[VMEM, HBM, HBM],
        out_specs=(VMEM,) * 5,
        scratch_shapes=[pltpu.SemaphoreType.DMA((2,))],
        compiler_params=params(),
        cost_estimate=cost(2 * 32 * rows * width * width, 10 * rows * channels),
        name="obs_tables",
    )(obs, in_hbm(own), in_hbm(columns))


def observe_kernel(
    own_ref,
    one_ref,
    two_ref,
    three_ref,
    slots_ref,
    jac_ref,
    w_ref,
    b_ref,
    channel_ref,
    adj_ref,
    evolved_ref,
):
    groups, rows, width = w_ref.shape
    state = jac_ref.shape[0]
    slots, owners = slots_ref.shape
    total = own_ref[...].astype(F32)
    for part in (one_ref, two_ref, three_ref):
        total = total + part[...].astype(F32)
    increment = total.astype(BF16)
    columns = increment.shape[1]
    column_id = lax.broadcasted_iota(I32, (columns, rows), 0)
    table = jnp.concatenate([slots_ref[j : j + 1, :] for j in range(slots)], axis=1)
    hits = jnp.where(column_id == jnp.broadcast_to(table, (columns, rows)), 1.0, 0.0)
    hits = hits.astype(BF16)
    carried = mm(increment, hits).T.astype(BF16)
    column_adjoint = jnp.zeros((rows, state), F32)
    channel = channel_ref[...]
    group, lane = channel >> 7, channel & 127
    picked = jnp.zeros(channel.shape, F32)
    for g in range(groups):
        jac = jac_ref[:, g * width : (g + 1) * width]
        model = mm(carried, jac)
        channel_adjoint = (model * w_ref[g] - b_ref[g]).astype(BF16)
        column_adjoint = column_adjoint + mm_nt(channel_adjoint, jac)
        taken = jnp.take_along_axis(model, lane, axis=1)
        picked = jnp.where(group == g, taken, picked)
    rounded = column_adjoint.T.astype(BF16)
    adj_ref[...] = mm_nt(rounded, hits).astype(BF16)
    for j in range(slots):
        evolved_ref[:, j, :] = picked[j * owners : (j + 1) * owners]


def observe(pieces, slots, jacobian, w_table, b_table, channel):
    state, width = pieces[0].shape
    channels = jacobian.shape[1]
    rows = channel.shape[0]
    return pl.pallas_call(
        observe_kernel,
        out_shape=(
            jax.ShapeDtypeStruct((state, width), BF16),
            jax.ShapeDtypeStruct((slots.shape[1], slots.shape[0], width), F32),
        ),
        in_specs=[VMEM] * 9,
        out_specs=(VMEM, VMEM),
        compiler_params=params(),
        cost_estimate=cost(4 * rows * state * channels, 12 * rows * channels),
        name="observe",
    )(*pieces, slots, jacobian, w_table, b_table, channel)


def member_adjoint_kernel(
    scale,
    place_ref,
    ens_hbm,
    own_ref,
    one_ref,
    two_ref,
    three_ref,
    full_hbm,
    low_hbm,
    high_hbm,
    ens_ref,
    adj_ref,
    full_ref,
    low_ref,
    high_ref,
    sems,
    full_sems,
    low_sems,
    high_sems,
):
    members, variables, levels, _ = ens_ref.shape
    blocks, width = adj_ref.shape[0], adj_ref.shape[3]
    half_blocks = blocks // 2
    step = LEVEL_STEP
    load = level_copies(ens_hbm, ens_ref, sems)
    for turn in range(levels // step):
        load(turn).start()

    mine = place_ref[2]
    for back, part in enumerate((own_ref, one_ref, two_ref, three_ref)):
        adj_ref[lax.rem(mine + blocks - back, blocks)] = part[...]

    def saves(turn):
        at = pl.ds(turn * step, step)
        return [
            pltpu.make_async_copy(source.at[:, at, :], target.at[:, at, :], sem.at[turn])
            for source, target, sem in (
                (low_ref, low_hbm, low_sems),
                (high_ref, high_hbm, high_sems),
                (full_ref, full_hbm, full_sems),
            )
        ]

    def one(turn, carry):
        at = pl.ds(pl.multiple_of(turn * step, step), step)
        load(turn).wait()
        for k in range(blocks):
            adjoint = [adj_ref[k, v, at, :].astype(F32) * scale for v in range(variables)]
            half = low_ref if k < half_blocks else high_ref
            offset = (k % half_blocks) * width
            for m in range(members):
                total = None
                for v in range(variables):
                    term = ens_ref[m, v, at, k * width : (k + 1) * width].astype(F32) * adjoint[v]
                    total = term if total is None else total + term
                full_ref[m, at, k * width : (k + 1) * width] = total
                half[m, at, offset : offset + width] = total.astype(BF16)
        for copy in saves(turn):
            copy.start()
        return carry

    lax.fori_loop(0, levels // step, one, 0)
    for turn in range(levels // step):
        for copy in saves(turn):
            copy.wait()


def member_adjoint(place, ensemble, pieces, scale):
    members, variables, levels, columns = ensemble.shape
    width = pieces[0].shape[-1]
    half = pltpu.HBM((members, levels, HALF), BF16)
    turns = pltpu.SemaphoreType.DMA((levels // LEVEL_STEP,))
    return pl.pallas_call(
        functools.partial(member_adjoint_kernel, scale),
        out_shape=(pltpu.HBM((members, levels, columns), F32), half, half),
        in_specs=[SMEM, HBM, VMEM, VMEM, VMEM, VMEM],
        out_specs=(HBM, HBM, HBM),
        scratch_shapes=[
            pltpu.VMEM(ensemble.shape, BF16),
            pltpu.VMEM((columns // width, variables, levels, width), BF16),
            pltpu.VMEM((members, levels, columns), F32),
            pltpu.VMEM((members, levels, HALF), BF16),
            pltpu.VMEM((members, levels, HALF), BF16),
            turns,
            turns,
            turns,
            turns,
        ],
        compiler_params=params(),
        cost_estimate=cost(2 * ensemble.size, 4 * ensemble.size),
        name="member_adjoint",
    )(place, in_hbm(ensemble), *pieces)


def add_halo_kernel(own_ref, low_ref, high_ref, t_ref, o_ref):
    i = pl.program_id(0)
    members = o_ref.shape[0]
    levels = o_ref.shape[1]
    rows = members * levels
    at = pl.ds(i * members, members)

    def from_halo(halo_ref, index):
        halo = mm(halo_ref[at].reshape(rows, HALF), t_ref[index]) * SWEEP_SCALE
        return halo.reshape(members, levels, HALF)

    o_ref[:, :, :HALF] = own_ref[at, :, :HALF] + from_halo(low_ref, 3)
    o_ref[:, :, HALF:] = own_ref[at, :, HALF:] + from_halo(high_ref, 4)


def add_halo(own, from_low, from_high, matrices):
    members, levels, columns = own.shape
    step = 4
    return pl.pallas_call(
        add_halo_kernel,
        out_shape=jax.ShapeDtypeStruct(own.shape, F32),
        grid=(members // step,),
        in_specs=[VMEM] * 4,
        out_specs=pl.BlockSpec((step, levels, columns), lambda i: (i, 0, 0)),
        compiler_params=params(),
        cost_estimate=cost(2 * own.size * HALF, 10 * own.size),
        name="add_halo",
    )(own, in_vmem(from_low), in_vmem(from_high), matrices)


def to_members(pieces):
    count = lax.axis_size("mem")
    received = []
    for shift, piece in enumerate(pieces, 1):
        pairs = [(i, (i + shift) % count) for i in range(count)]
        received.append(lax.ppermute(piece, "mem", pairs))
    return received


def keep_kernel(count_ref, innovation_ref, o_ref):
    owners, slots, observed = innovation_ref.shape
    slot_id = lax.broadcasted_iota(I32, (slots, observed), 0)
    for s in range(owners):
        o_ref[s] = jnp.where(slot_id < count_ref[0, s], innovation_ref[s], 0.0)


def keep_filled(counts, innovation):
    return pl.pallas_call(
        keep_kernel,
        out_shape=jax.ShapeDtypeStruct(innovation.shape, F32),
        in_specs=[SMEM, VMEM],
        out_specs=VMEM,
        compiler_params=params(),
        cost_estimate=cost(innovation.size, 8 * innovation.size),
        name="keep_filled",
    )(counts, innovation)


def swap_halos(low_half, high_half):
    count = lax.axis_size("tile")
    forward = [(i, i + 1) for i in range(count - 1)]
    backward = [(i + 1, i) for i in range(count - 1)]
    from_low = lax.ppermute(high_half, "tile", forward)
    from_high = lax.ppermute(low_half, "tile", backward)
    return from_low, from_high


def body(
    control,
    ensemble,
    jacobian,
    send_columns,
    received_counts,
    observed_channel,
    innovation,
    error_weight,
):
    members, levels, columns = control.shape
    variables = ensemble.shape[1]
    state = variables * levels
    groups = lax.axis_size("mem")
    owners = lax.axis_size("tile")
    scale = 1.0 / math.sqrt(members * groups)
    width = columns // groups
    channels = jacobian.shape[0]
    tile_index = lax.axis_index("tile")
    matrices = jnp.asarray(sweep_matrices())
    place = jnp.stack(
        [
            jnp.where(tile_index == 0, 0, 1),
            jnp.where(tile_index == owners - 1, 2, 1),
            lax.axis_index("mem"),
        ]
    ).astype(I32)
    counts = received_counts
    low_half, high_half, packed = encode(
        counts, control, observed_channel[0], innovation[0], error_weight[0]
    )
    from_low, from_high = swap_halos(low_half, high_half)
    obs = lax.all_to_all(packed, "tile", split_axis=0, concat_axis=0, tiled=True)
    pieces = localize_sum(place, control, from_low, from_high, ensemble, matrices, scale, groups)
    pieces = [piece.reshape(state, width) for piece in pieces]
    received = to_members(pieces[1:])
    w_table, b_table, channel, own, carried = obs_tables(
        obs, pieces[0], jnp.transpose(send_columns[0]), channels
    )
    block_adjoint, evolved = observe(
        [own] + received,
        carried,
        jnp.transpose(jacobian),
        w_table,
        b_table,
        channel,
    )
    adjoint = [block_adjoint] + to_members([block_adjoint] * (groups - 1))
    adjoint = [piece.reshape(variables, levels, width) for piece in adjoint]
    evolved = lax.all_to_all(evolved, "tile", split_axis=0, concat_axis=0, tiled=True)
    kept = keep_filled(counts, innovation[0])
    full, low_half, high_half = member_adjoint(place, ensemble, adjoint, scale)
    from_low, from_high = swap_halos(low_half, high_half)
    own = sweep_own(place, full.reshape(members * levels, columns), matrices, True)
    departures = depart(counts, evolved, kept)
    gradient = add_halo(
        own.reshape(members, levels, columns), from_low, from_high, matrices
    )
    return gradient, departures[None]


def solution(mesh):
    in_specs = (
        P("mem", None, "tile"),
        P("mem", None, None, "tile"),
        P(),
        P(("tile", "mem"), None, None),
        P(("tile", "mem"), None),
        P(("tile", "mem"), None, None, None),
        P(("tile", "mem"), None, None, None),
        P(("tile", "mem"), None, None, None),
    )
    out_specs = (P("mem", None, "tile"), P(("tile", "mem"), None, None, None))
    return jax.shard_map(body, mesh=mesh, in_specs=in_specs, out_specs=out_specs, check_vma=False)
```

```python
import functools
import math

import jax
import jax.numpy as jnp
import numpy as np
from jax import lax
from jax.experimental import pallas as pl
from jax.experimental.pallas import tpu as pltpu
from jax.sharding import PartitionSpec as P


NY = 64
SWEEPS = 4
SWEEP_SCALE = 0.2**SWEEPS
HALF = SWEEPS * NY

CONTROL_STEP = 2.0**-12
INNOVATION_STEP = 1.5 / 32700.0
WEIGHT_STEP = 10.0 / 32700.0

F32 = jnp.float32
BF16 = jnp.bfloat16
I16 = jnp.int16
I32 = jnp.int32

VMEM = pl.BlockSpec(memory_space=pltpu.VMEM)
HBM = pl.BlockSpec(memory_space=pltpu.HBM)
SMEM = pl.BlockSpec(memory_space=pltpu.SMEM)


def sweep_matrices():
    y_part = np.eye(NY) + np.eye(NY, k=1) + np.eye(NY, k=-1)
    powers = [np.linalg.matrix_power(y_part, n) for n in range(SWEEPS + 1)]
    by_distance = [np.zeros((NY, NY)) for _ in range(SWEEPS + 1)]
    for k in range(SWEEPS + 1):
        for ups in range(k + 1):
            distance = 2 * ups - k
            if distance >= 0:
                by_distance[distance] = (
                    by_distance[distance]
                    + math.comb(SWEEPS, k) * math.comb(k, ups) * powers[SWEEPS - k]
                )

    def block(distance_of, image_of=None):
        full = np.zeros((HALF, HALF))
        for xi in range(SWEEPS):
            for xo in range(SWEEPS):
                piece = np.zeros((NY, NY))
                if distance_of(xi, xo) <= SWEEPS:
                    piece = piece + by_distance[distance_of(xi, xo)]
                if image_of is not None and image_of(xi, xo) <= SWEEPS:
                    piece = piece - by_distance[image_of(xi, xo)]
                full[xi * NY : (xi + 1) * NY, xo * NY : (xo + 1) * NY] = piece
        return full

    last = SWEEPS - 1
    same = lambda xi, xo: abs(xi - xo)
    blocks = [
        block(same, lambda xi, xo: xi + xo + 2),
        block(same),
        block(same, lambda xi, xo: (last - xi) + (last - xo) + 2),
        block(lambda xi, xo: xo + SWEEPS - xi),
        block(lambda xi, xo: xi + SWEEPS - xo),
    ]
    return np.stack(blocks).astype(jnp.bfloat16)


def split_high_low(values):
    high = values.astype(BF16)
    return high, (values - high.astype(F32)).astype(BF16)


def mm(a, b):
    return jnp.dot(a, b, preferred_element_type=F32)


def mm_nt(a, b):
    return lax.dot_general(a, b, (((1,), (1,)), ((), ())), preferred_element_type=F32)


def in_vmem(x):
    return pltpu.with_memory_space_constraint(x, pltpu.VMEM)


def in_hbm(x):
    return pltpu.with_memory_space_constraint(x, pltpu.HBM)


def params(**extra):
    return pltpu.CompilerParams(vmem_limit_bytes=24 * 1024 * 1024, **extra)


def cost(flops, bytes_accessed):
    return pl.CostEstimate(flops=flops, bytes_accessed=bytes_accessed, transcendentals=0)


ENCODE_STEP = 2


def encode_kernel(
    count_hbm,
    x_hbm,
    channel_hbm,
    innovation_hbm,
    weight_hbm,
    low_hbm,
    high_hbm,
    packed_hbm,
    count_ref,
    x_ref,
    channel_ref,
    innovation_ref,
    weight_ref,
    low_ref,
    high_ref,
    packed_ref,
    in_sems,
    obs_sems,
    low_sems,
    high_sems,
    packed_sem,
):
    turns = x_hbm.shape[0] // ENCODE_STEP
    owners, slots, observed = channel_hbm.shape

    def chunk(source, target, sems, turn):
        at = pl.ds(turn * ENCODE_STEP, ENCODE_STEP)
        return pltpu.make_async_copy(source.at[at], target.at[at], sems.at[turn])

    obs_loads = [
        pltpu.make_async_copy(count_hbm, count_ref, obs_sems.at[3]),
        pltpu.make_async_copy(channel_hbm, channel_ref, obs_sems.at[0]),
        pltpu.make_async_copy(innovation_hbm, innovation_ref, obs_sems.at[1]),
        pltpu.make_async_copy(weight_hbm, weight_ref, obs_sems.at[2]),
    ]
    for turn in range(turns - 1):
        chunk(x_hbm, x_ref, in_sems, turn).start()
    for copy in obs_loads:
        copy.start()
    chunk(x_hbm, x_ref, in_sems, turns - 1).start()
    saves = []

    def encode_chunk(turn):
        chunk(x_hbm, x_ref, in_sems, turn).wait()
        at = slice(turn * ENCODE_STEP, (turn + 1) * ENCODE_STEP)
        coded = jnp.minimum(jnp.round(x_ref[at] * (1.0 / CONTROL_STEP)), 32767.0)
        coded = coded.astype(I32).astype(I16)
        low_ref[at] = coded[:, :, :HALF]
        high_ref[at] = coded[:, :, HALF:]
        for source, target, sems in (
            (low_ref, low_hbm, low_sems),
            (high_ref, high_hbm, high_sems),
        ):
            saves.append(chunk(source, target, sems, turn))
            saves[-1].start()

    for turn in range(turns - 1):
        encode_chunk(turn)
    for copy in obs_loads:
        copy.wait()
    slot_id = lax.broadcasted_iota(I32, (slots, observed), 0)
    for s in range(owners):
        filled = slot_id < count_ref[0, s]
        weight = jnp.where(filled, weight_ref[s] * (1.0 / WEIGHT_STEP), 0.0)
        innovation = innovation_ref[s] * (1.0 / INNOVATION_STEP)
        row = [channel_ref[s], jnp.round(innovation).astype(I32), jnp.round(weight).astype(I32)]
        for n, values in enumerate(row):
            packed_ref[s, :, n * observed : (n + 1) * observed] = values.astype(I16)
    saves.append(pltpu.make_async_copy(packed_ref, packed_hbm, packed_sem))
    saves[-1].start()
    encode_chunk(turns - 1)
    for copy in saves:
        copy.wait()


def encode(counts, control, channel, innovation, weight):
    members, levels, _ = control.shape
    owners, slots, observed = channel.shape
    turns = members // ENCODE_STEP
    half = (members, levels, HALF)
    packed = (owners, slots, 3 * observed)
    return pl.pallas_call(
        encode_kernel,
        out_shape=(pltpu.HBM(half, I16), pltpu.HBM(half, I16), pltpu.HBM(packed, I16)),
        in_specs=[HBM] * 5,
        out_specs=(HBM, HBM, HBM),
        scratch_shapes=[
            pltpu.SMEM(counts.shape, I32),
            pltpu.VMEM(control.shape, F32),
            pltpu.VMEM(channel.shape, I32),
            pltpu.VMEM(channel.shape, F32),
            pltpu.VMEM(channel.shape, F32),
            pltpu.VMEM(half, I16),
            pltpu.VMEM(half, I16),
            pltpu.VMEM(packed, I16),
            pltpu.SemaphoreType.DMA((turns,)),
            pltpu.SemaphoreType.DMA((4,)),
            pltpu.SemaphoreType.DMA((turns,)),
            pltpu.SemaphoreType.DMA((turns,)),
            pltpu.SemaphoreType.DMA,
        ],
        compiler_params=params(),
        cost_estimate=cost(4 * control.size, 6 * control.size),
        name="encode",
    )(*[in_hbm(x) for x in (counts, control, channel, innovation, weight)])


def depart_kernel(count_ref, evolved_ref, innovation_ref, o_ref):
    owners, slots, observed = evolved_ref.shape
    slot_id = lax.broadcasted_iota(I32, (slots, observed), 0)
    for s in range(owners):
        filled = slot_id < count_ref[0, s]
        o_ref[s] = jnp.where(filled, evolved_ref[s], 0.0) - innovation_ref[s]


def depart(counts, evolved, innovation):
    return pl.pallas_call(
        depart_kernel,
        out_shape=jax.ShapeDtypeStruct(evolved.shape, F32),
        in_specs=[SMEM, VMEM, VMEM],
        out_specs=VMEM,
        compiler_params=params(),
        cost_estimate=cost(2 * evolved.size, 12 * evolved.size),
        name="depart",
    )(counts, evolved, innovation)


def sweep_own_kernel(place_ref, x_ref, t_ref, o_ref):
    members, levels, _ = x_ref.shape
    step = 4
    rows = step * levels

    def one(turn, carry):
        at = pl.ds(turn * step, step)
        left_high, left_low = split_high_low(x_ref[at, :, :HALF].reshape(rows, HALF))
        right_high, right_low = split_high_low(x_ref[at, :, HALF:].reshape(rows, HALF))

        def apply(high, low, index):
            return mm(high, t_ref[index]) + mm(low, t_ref[index])

        left = apply(left_high, left_low, place_ref[0]) + apply(right_high, right_low, 4)
        right = apply(right_high, right_low, place_ref[1]) + apply(left_high, left_low, 3)
        shape = (step, levels, HALF)
        o_ref[at, :, :HALF] = (left * SWEEP_SCALE).reshape(shape)
        o_ref[at, :, HALF:] = (right * SWEEP_SCALE).reshape(shape)
        return carry

    lax.fori_loop(0, members // step, one, 0)


def sweep_own(place, field, matrices):
    return pl.pallas_call(
        sweep_own_kernel,
        out_shape=jax.ShapeDtypeStruct(field.shape, F32),
        in_specs=[SMEM, VMEM, VMEM],
        out_specs=VMEM,
        compiler_params=params(),
        cost_estimate=cost(2 * 4 * field.size * HALF, 10 * field.size),
        name="sweep_own",
    )(place, in_vmem(field), matrices)


LEVEL_STEP = 16


def level_copies(source, target, sems):
    def copy(turn):
        at = pl.ds(turn * LEVEL_STEP, LEVEL_STEP)
        return pltpu.make_async_copy(
            source.at[:, :, at, :], target.at[:, :, at, :], sems.at[turn]
        )

    return copy


def localize_sum_kernel(
    scale,
    place_ref,
    x_ref,
    low_ref,
    high_ref,
    ens_hbm,
    t_hbm,
    own_hbm,
    one_hbm,
    two_hbm,
    three_hbm,
    ens_ref,
    t_ref,
    near_left,
    near_right,
    w_left,
    w_right,
    o_ref,
    in_sems,
    t_sem,
    out_sems,
):
    members, variables, levels, _ = ens_ref.shape
    blocks, width = o_ref.shape[0], o_ref.shape[3]
    step = LEVEL_STEP
    turns = levels // step
    load = level_copies(ens_hbm, ens_ref, in_sems)
    t_load = pltpu.make_async_copy(t_hbm, t_ref, t_sem)
    t_load.start()
    for turn in range(turns):
        load(turn).start()

    def twice(index):
        return jnp.concatenate([t_ref[index], t_ref[index]], axis=0)

    rows = step * members
    group = members // 2
    half_rows = step * group

    def pair_of(values):
        return jnp.concatenate(split_high_low(values), axis=1)

    def split_near(turn):
        at = pl.ds(pl.multiple_of(turn * step, step), step)
        near_left[...] = pair_of(x_ref[:, at, :HALF].reshape(rows, HALF))
        near_right[...] = pair_of(x_ref[:, at, HALF:].reshape(rows, HALF))

    def weigh(turn, right_side, piece):
        at = pl.ds(pl.multiple_of(turn * step, step), step)
        among = slice(piece * group, (piece + 1) * group)
        these = slice(piece * half_rows, (piece + 1) * half_rows)
        left, right = near_left[these], near_right[these]
        halo_ref, w_ref = (high_ref, w_right) if right_side else (low_ref, w_left)
        beyond = halo_ref[among, at, :].reshape(half_rows, HALF).astype(I32).astype(F32)
        beyond = pair_of(beyond)
        if right_side:
            new = mm(right, twice(place_ref[1])) + mm(left, twice(3)) + mm(beyond, twice(6))
        else:
            new = mm(left, twice(place_ref[0])) + mm(right, twice(4)) + mm(beyond, twice(5))
        w_ref[among] = (new * SWEEP_SCALE).astype(BF16).reshape(group, step, HALF)

    def total_up(turn, w_ref, k):
        at = pl.ds(pl.multiple_of(turn * step, step), step)
        across = slice(k * width, (k + 1) * width)
        within = slice(k * width % HALF, k * width % HALF + width)
        totals = [None] * variables
        for m in range(members):
            weight = w_ref[m, :, within].astype(F32)
            for v in range(variables):
                term = weight * ens_ref[m, v, at, across].astype(F32)
                totals[v] = term if totals[v] is None else totals[v] + term
        for v in range(variables):
            o_ref[k, v, at, :] = (totals[v] * scale).astype(BF16)

    split_near(0)
    t_load.wait()
    for piece in range(2):
        weigh(0, False, piece)

    def one(turn, carry):
        load(turn).wait()
        for piece in range(2):
            weigh(turn, True, piece)
            total_up(turn, w_left, piece)
        later = jnp.minimum(turn + 1, turns - 1)
        split_near(later)
        for piece in range(2):
            weigh(later, False, piece)
            total_up(turn, w_right, blocks // 2 + piece)
        return carry

    lax.fori_loop(0, turns, one, 0)
    mine = place_ref[2]
    copies = [
        pltpu.make_async_copy(o_ref.at[lax.rem(mine + s, blocks)], target, out_sems.at[s])
        for s, target in enumerate((own_hbm, one_hbm, two_hbm, three_hbm))
    ]
    for copy in copies:
        copy.start()
    for copy in copies:
        copy.wait()


def localize_sum(place, control, from_low, from_high, ensemble, matrices, scale, blocks):
    members, variables, levels, columns = ensemble.shape
    width = columns // blocks
    turns = levels // LEVEL_STEP
    piece = pltpu.HBM((variables, levels, width), BF16)
    return pl.pallas_call(
        functools.partial(localize_sum_kernel, scale),
        out_shape=(piece,) * blocks,
        in_specs=[SMEM, VMEM, VMEM, VMEM, HBM, HBM],
        out_specs=(HBM,) * blocks,
        scratch_shapes=[
            pltpu.VMEM(ensemble.shape, BF16),
            pltpu.VMEM(matrices.shape, BF16),
            pltpu.VMEM((members * LEVEL_STEP, 2 * HALF), BF16),
            pltpu.VMEM((members * LEVEL_STEP, 2 * HALF), BF16),
            pltpu.VMEM((members, LEVEL_STEP, HALF), BF16),
            pltpu.VMEM((members, LEVEL_STEP, HALF), BF16),
            pltpu.VMEM((blocks, variables, levels, width), BF16),
            pltpu.SemaphoreType.DMA((turns,)),
            pltpu.SemaphoreType.DMA,
            pltpu.SemaphoreType.DMA((blocks,)),
        ],
        compiler_params=params(),
        cost_estimate=cost(
            2 * 6 * members * levels * columns * HALF, 2 * ensemble.size + 8 * control.size
        ),
        name="localize_sum",
    )(
        place,
        in_vmem(control),
        in_vmem(from_low),
        in_vmem(from_high),
        in_hbm(ensemble),
        in_hbm(matrices),
    )


def obs_tables_kernel(
    obs_ref, own_hbm, slots_hbm, w_ref, b_ref, channel_ref, own_ref, hits_ref, slots_ref, sems
):
    copies = [
        pltpu.make_async_copy(own_hbm, own_ref, sems.at[0]),
        pltpu.make_async_copy(slots_hbm, slots_ref, sems.at[1]),
    ]
    for copy in copies:
        copy.start()
    owners, slots, _ = obs_ref.shape
    groups, _, width = w_ref.shape
    group_id = lax.broadcasted_iota(I32, (8, width), 0)
    lane_id = lax.broadcasted_iota(I32, (width, width), 0).astype(F32).astype(BF16)
    one_bf, zero_bf = jnp.ones((), BF16), jnp.zeros((), BF16)

    zeros = jnp.zeros((32, width), BF16)

    def prepare(owner, slot):
        row = obs_ref[owner].astype(I32)[slot : slot + 1]
        channel = row[:, :width]
        innovation = row[:, width : 2 * width].astype(F32) * INNOVATION_STEP
        weight = row[:, 2 * width :].astype(F32) * WEIGHT_STEP
        in_group = jnp.broadcast_to(channel >> 7, (8, width)) == group_id
        lane = (channel & 127).astype(F32).astype(BF16)
        one_hot = jnp.where(jnp.broadcast_to(lane, (width, width)) == lane_id, one_bf, zero_bf)

        def spread(values):
            return [
                jnp.where(in_group, jnp.broadcast_to(part.astype(F32), (8, width)), 0.0)
                for part in split_high_low(values)
            ]

        left = jnp.concatenate(spread(weight) + spread(weight * innovation), axis=0)
        return channel, one_hot, left.astype(BF16)

    def pair(owner):
        first, second = prepare(owner, 0), prepare(owner, 1)
        left = jnp.concatenate(
            [
                jnp.concatenate([first[2], zeros], axis=1),
                jnp.concatenate([zeros, second[2]], axis=1),
            ],
            axis=0,
        )
        one_hot = jnp.concatenate([first[1], second[1]], axis=1)
        both = mm_nt(left, one_hot)
        for slot, channel in enumerate((first[0], second[0])):
            sums = both[32 * slot : 32 * (slot + 1)]
            w_sum = sums[0:8] + sums[8:16]
            b_sum = sums[16:24] + sums[24:32]
            at = pl.ds(slot * owners + owner, 1)
            channel_ref[at, :] = channel
            for g in range(groups):
                w_ref[g, at, :] = w_sum[g : g + 1]
                b_ref[g, at, :] = b_sum[g : g + 1]

    unroll = 16

    def several(turn, carry):
        for inner in range(unroll):
            pair(turn * unroll + inner)
        return carry

    lax.fori_loop(0, owners // unroll, several, 0)
    for copy in copies:
        copy.wait()
    table = jnp.concatenate([slots_ref[j : j + 1, :] for j in range(slots)], axis=1)
    columns, rows = hits_ref.shape[1:]
    column_id = lax.broadcasted_iota(I32, (columns, rows), 0)
    hits = jnp.where(column_id == jnp.broadcast_to(table, (columns, rows)), 1.0, 0.0)
    hits_ref[0] = hits.astype(BF16)
    hits_ref[1] = hits.T.astype(BF16)


def obs_tables(obs, own, columns, channels):
    owners, slots, packed = obs.shape
    width = packed // 3
    rows = owners * slots
    shape = jax.ShapeDtypeStruct((channels // width, rows, width), F32)
    return pl.pallas_call(
        obs_tables_kernel,
        out_shape=(
            shape,
            shape,
            jax.ShapeDtypeStruct((rows, width), I32),
            jax.ShapeDtypeStruct(own.shape, own.dtype),
            jax.ShapeDtypeStruct((2, own.shape[1], rows), BF16),
        ),
        in_specs=[VMEM, HBM, HBM],
        out_specs=(VMEM,) * 5,
        scratch_shapes=[pltpu.VMEM(columns.shape, I32), pltpu.SemaphoreType.DMA((2,))],
        compiler_params=params(),
        cost_estimate=cost(2 * 32 * rows * width * width, 10 * rows * channels),
        name="obs_tables",
    )(obs, in_hbm(own), in_hbm(columns))


def observe_kernel(
    own_ref,
    one_ref,
    two_ref,
    three_ref,
    hits_ref,
    jac_ref,
    w_ref,
    b_ref,
    channel_ref,
    adj_ref,
    evolved_ref,
):
    groups, rows, width = w_ref.shape
    state = jac_ref.shape[0]
    owners, slots, _ = evolved_ref.shape
    total = own_ref[...].astype(F32)
    for part in (one_ref, two_ref, three_ref):
        total = total + part[...].astype(F32)
    increment = total.astype(BF16)
    carried = mm_nt(hits_ref[1], increment).astype(BF16)
    column_adjoint = jnp.zeros((rows, state), F32)
    channel = channel_ref[...]
    group, lane = channel >> 7, channel & 127
    picked = jnp.zeros(channel.shape, F32)
    for g in range(groups):
        jac = jac_ref[:, g * width : (g + 1) * width]
        model = mm(carried, jac)
        channel_adjoint = (model * w_ref[g] - b_ref[g]).astype(BF16)
        column_adjoint = column_adjoint + mm_nt(channel_adjoint, jac)
        taken = jnp.take_along_axis(model, lane, axis=1)
        picked = jnp.where(group == g, taken, picked)
    rounded = column_adjoint.T.astype(BF16)
    adj_ref[...] = mm_nt(rounded, hits_ref[0]).astype(BF16)
    for j in range(slots):
        evolved_ref[:, j, :] = picked[j * owners : (j + 1) * owners]


def observe(pieces, hits, jacobian, w_table, b_table, channel, owners):
    state, width = pieces[0].shape
    channels = jacobian.shape[1]
    rows = channel.shape[0]
    return pl.pallas_call(
        observe_kernel,
        out_shape=(
            jax.ShapeDtypeStruct((state, width), BF16),
            jax.ShapeDtypeStruct((owners, rows // owners, width), F32),
        ),
        in_specs=[VMEM] * 9,
        out_specs=(VMEM, VMEM),
        compiler_params=params(),
        cost_estimate=cost(4 * rows * state * channels, 12 * rows * channels),
        name="observe",
    )(*pieces, hits, jacobian, w_table, b_table, channel)


def member_adjoint_kernel(
    scale,
    place_ref,
    ens_hbm,
    own_ref,
    one_ref,
    two_ref,
    three_ref,
    full_hbm,
    low_hbm,
    high_hbm,
    ens_ref,
    adj_ref,
    full_ref,
    low_ref,
    high_ref,
    sems,
    full_sems,
    low_sems,
    high_sems,
):
    members, variables, levels, _ = ens_ref.shape
    blocks, width = adj_ref.shape[0], adj_ref.shape[3]
    half_blocks = blocks // 2
    step = LEVEL_STEP
    load = level_copies(ens_hbm, ens_ref, sems)
    for turn in range(levels // step):
        load(turn).start()

    mine = place_ref[2]
    for back, part in enumerate((own_ref, one_ref, two_ref, three_ref)):
        adj_ref[lax.rem(mine + blocks - back, blocks)] = part[...]

    def saves(turn):
        at = pl.ds(turn * step, step)
        return [
            pltpu.make_async_copy(source.at[:, at, :], target.at[:, at, :], sem.at[turn])
            for source, target, sem in (
                (low_ref, low_hbm, low_sems),
                (high_ref, high_hbm, high_sems),
                (full_ref, full_hbm, full_sems),
            )
        ]

    def one(turn, carry):
        at = pl.ds(pl.multiple_of(turn * step, step), step)
        load(turn).wait()
        for k in range(blocks):
            adjoint = [adj_ref[k, v, at, :].astype(F32) * scale for v in range(variables)]
            half = low_ref if k < half_blocks else high_ref
            offset = (k % half_blocks) * width
            for m in range(members):
                total = None
                for v in range(variables):
                    term = ens_ref[m, v, at, k * width : (k + 1) * width].astype(F32) * adjoint[v]
                    total = term if total is None else total + term
                full_ref[m, at, k * width : (k + 1) * width] = total
                half[m, at, offset : offset + width] = total.astype(BF16)
        for copy in saves(turn):
            copy.start()
        return carry

    lax.fori_loop(0, levels // step, one, 0)
    for turn in range(levels // step):
        for copy in saves(turn):
            copy.wait()


def member_adjoint(place, ensemble, pieces, scale):
    members, variables, levels, columns = ensemble.shape
    width = pieces[0].shape[-1]
    half = pltpu.HBM((members, levels, HALF), BF16)
    turns = pltpu.SemaphoreType.DMA((levels // LEVEL_STEP,))
    return pl.pallas_call(
        functools.partial(member_adjoint_kernel, scale),
        out_shape=(pltpu.HBM((members, levels, columns), F32), half, half),
        in_specs=[SMEM, HBM, VMEM, VMEM, VMEM, VMEM],
        out_specs=(HBM, HBM, HBM),
        scratch_shapes=[
            pltpu.VMEM(ensemble.shape, BF16),
            pltpu.VMEM((columns // width, variables, levels, width), BF16),
            pltpu.VMEM((members, levels, columns), F32),
            pltpu.VMEM((members, levels, HALF), BF16),
            pltpu.VMEM((members, levels, HALF), BF16),
            turns,
            turns,
            turns,
            turns,
        ],
        compiler_params=params(),
        cost_estimate=cost(2 * ensemble.size, 4 * ensemble.size),
        name="member_adjoint",
    )(place, in_hbm(ensemble), *pieces)


def add_halo_kernel(
    own_ref, low_ref, high_hbm, t_ref, o_hbm, high_ref, o_ref, high_sem, low_sems, high_sems
):
    members, levels, _ = own_ref.shape
    step = 4
    rows = step * levels
    turns = members // step
    load = pltpu.make_async_copy(high_hbm, high_ref, high_sem)
    load.start()

    def save(turn, across, sems):
        at = pl.ds(turn * step, step)
        return pltpu.make_async_copy(
            o_ref.at[at, :, across], o_hbm.at[at, :, across], sems.at[turn]
        )

    def half(halo_ref, across, index, sems):
        def one(turn, carry):
            at = pl.ds(turn * step, step)
            halo = mm(halo_ref[at].reshape(rows, HALF), t_ref[index]) * SWEEP_SCALE
            o_ref[at, :, across] = own_ref[at, :, across] + halo.reshape(step, levels, HALF)
            save(turn, across, sems).start()
            return carry

        lax.fori_loop(0, turns, one, 0)

    lower, upper = pl.ds(0, HALF), pl.ds(HALF, HALF)
    half(low_ref, lower, 3, low_sems)
    load.wait()
    half(high_ref, upper, 4, high_sems)
    for turn in range(turns):
        save(turn, lower, low_sems).wait()
        save(turn, upper, high_sems).wait()


def add_halo(own, from_low, from_high, matrices):
    members = own.shape[0]
    return pl.pallas_call(
        add_halo_kernel,
        out_shape=pltpu.HBM(own.shape, F32),
        in_specs=[VMEM, VMEM, HBM, VMEM],
        out_specs=HBM,
        scratch_shapes=[
            pltpu.VMEM(from_high.shape, BF16),
            pltpu.VMEM(own.shape, F32),
            pltpu.SemaphoreType.DMA,
            pltpu.SemaphoreType.DMA((members // 4,)),
            pltpu.SemaphoreType.DMA((members // 4,)),
        ],
        compiler_params=params(),
        cost_estimate=cost(2 * own.size * HALF, 10 * own.size),
        name="add_halo",
    )(own, in_vmem(from_low), in_hbm(from_high), matrices)


def to_members(pieces):
    count = lax.axis_size("mem")
    received = []
    for shift, piece in enumerate(pieces, 1):
        pairs = [(i, (i + shift) % count) for i in range(count)]
        received.append(lax.ppermute(piece, "mem", pairs))
    return received


def keep_kernel(count_ref, innovation_ref, o_ref):
    owners, slots, observed = innovation_ref.shape
    slot_id = lax.broadcasted_iota(I32, (slots, observed), 0)
    for s in range(owners):
        o_ref[s] = jnp.where(slot_id < count_ref[0, s], innovation_ref[s], 0.0)


def keep_filled(counts, innovation):
    return pl.pallas_call(
        keep_kernel,
        out_shape=jax.ShapeDtypeStruct(innovation.shape, F32),
        in_specs=[SMEM, VMEM],
        out_specs=VMEM,
        compiler_params=params(),
        cost_estimate=cost(innovation.size, 8 * innovation.size),
        name="keep_filled",
    )(counts, innovation)


def swap_halos(low_half, high_half):
    count = lax.axis_size("tile")
    forward = [(i, i + 1) for i in range(count - 1)]
    backward = [(i + 1, i) for i in range(count - 1)]
    from_low = lax.ppermute(high_half, "tile", forward)
    from_high = lax.ppermute(low_half, "tile", backward)
    return from_low, from_high


def body(
    control,
    ensemble,
    jacobian,
    send_columns,
    received_counts,
    observed_channel,
    innovation,
    error_weight,
):
    members, levels, columns = control.shape
    variables = ensemble.shape[1]
    state = variables * levels
    groups = lax.axis_size("mem")
    owners = lax.axis_size("tile")
    scale = 1.0 / math.sqrt(members * groups)
    width = columns // groups
    channels = jacobian.shape[0]
    tile_index = lax.axis_index("tile")
    near = sweep_matrices()
    matrices = jnp.asarray(near)
    scaled = np.concatenate([near, (near[3:].astype(np.float32) * CONTROL_STEP).astype(near.dtype)])
    matrices_with_halo = jnp.asarray(scaled)
    place = jnp.stack(
        [
            jnp.where(tile_index == 0, 0, 1),
            jnp.where(tile_index == owners - 1, 2, 1),
            lax.axis_index("mem"),
        ]
    ).astype(I32)
    counts = received_counts
    low_half, high_half, packed = encode(
        counts, control, observed_channel[0], innovation[0], error_weight[0]
    )
    from_low, from_high = swap_halos(low_half, high_half)
    obs = lax.all_to_all(packed, "tile", split_axis=0, concat_axis=0, tiled=True)
    pieces = localize_sum(
        place, control, from_low, from_high, ensemble, matrices_with_halo, scale, groups
    )
    pieces = [piece.reshape(state, width) for piece in pieces]
    received = to_members(pieces[1:])
    w_table, b_table, channel, own, hits = obs_tables(
        obs, pieces[0], jnp.transpose(send_columns[0]), channels
    )
    block_adjoint, evolved = observe(
        [own] + received,
        hits,
        jnp.transpose(jacobian),
        w_table,
        b_table,
        channel,
        owners,
    )
    adjoint = [block_adjoint] + to_members([block_adjoint] * (groups - 1))
    adjoint = [piece.reshape(variables, levels, width) for piece in adjoint]
    evolved = lax.all_to_all(evolved, "tile", split_axis=0, concat_axis=0, tiled=True)
    kept = keep_filled(counts, innovation[0])
    full, low_half, high_half = member_adjoint(place, ensemble, adjoint, scale)
    from_low, from_high = swap_halos(low_half, high_half)
    own = sweep_own(place, full, matrices)
    departures = depart(counts, evolved, kept)
    gradient = add_halo(
        own, from_low, from_high, matrices
    )
    return gradient, departures[None]


def solution(mesh):
    in_specs = (
        P("mem", None, "tile"),
        P("mem", None, None, "tile"),
        P(),
        P(("tile", "mem"), None, None),
        P(("tile", "mem"), None),
        P(("tile", "mem"), None, None, None),
        P(("tile", "mem"), None, None, None),
        P(("tile", "mem"), None, None, None),
    )
    out_specs = (P("mem", None, "tile"), P(("tile", "mem"), None, None, None))
    return jax.shard_map(body, mesh=mesh, in_specs=in_specs, out_specs=out_specs, check_vma=False)
```
